512 devices in a mesh: rep: 8 (over y), dom: 64 (over x, z, core).
Axes of the slice: x: 4, y: 8, z: 8, core: 2. Of those that a mesh axis runs over, the one named last changes fastest.
Arguments:
- feats: bfloat16 [65536, 256], P(('rep', 'dom')), may hold values from -6 to 6
- w_self: bfloat16 [256, 256], replicated, may hold values from -0.375 to 0.375
- w_neigh: bfloat16 [256, 256], replicated, may hold values from -1.5 to 1.5
- tile_vals: bfloat16 [8, 64, 128, 128, 128], P('rep', 'dom'), may hold values from 0 to 1
- tile_owner: int32 [8, 64, 128], P('rep', 'dom'), may hold values from 0 to 63, as said below
- tile_src: int32 [8, 64, 128], P('rep', 'dom'), may hold values from 0 to 7
- tile_count: int32 [8, 64], P('rep', 'dom'), may hold values from 64 to 128, as said below
- d_out: bfloat16 [65536, 256], P(('rep', 'dom')), may hold values from -6 to 6
Outputs:
- out_feats: bfloat16 [65536, 256], P(('rep', 'dom'))
- d_feats: bfloat16 [65536, 256], P(('rep', 'dom'))
- grad_self: float32 [256, 256], P('dom')
- grad_neigh: float32 [256, 256], P('dom')
The draws below stay inside these ranges and needn't reach their ends.
Inputs may be any that keep to these rules, and one draw needn't show every extreme that they name: Within one list no two tiles name the same pair of tile_owner and tile_src. Tiles of list (i, j) at positions tile_count[i, j] and beyond are padding.
All inputs are finite; a program needn't handle non-finite values.
Results may differ from the reference program's by a relative error of at most 0.0049.
Values may be sent and summed in bfloat16 or wider, within the bound.
No kernel may reach another device: no remote copies, remote signals or barrier semaphores. Data moves between devices by JAX's collectives and lax.ppermute only.
A program may use at most 128 MiB of HBM per device.

```python
import jax
import jax.numpy as jnp
from jax import lax

HID = 256
TILE = 128
ROWS = 128
TILES = 128
NODES = 65536
N_REP = 8
N_DOM = 64


def tile_places(key):
    per_block = ROWS // TILE
    total = N_DOM * per_block * N_REP * per_block
    keys = jax.random.split(jax.random.fold_in(key, 7), N_REP * N_DOM)
    picked = jax.vmap(lambda one_key: jax.random.permutation(one_key, total)[:TILES])(keys)
    return picked.reshape(N_REP, N_DOM, TILES).astype(jnp.int32)


def draw_tile_owner(key, part):
    return (tile_places(key) // (N_REP * (ROWS // TILE))).astype(jnp.int32)


def draw_tile_src(key, part):
    return (tile_places(key) % (N_REP * (ROWS // TILE))).astype(jnp.int32)


def draw_tile_count(key, part):
    keys = jax.random.split(jax.random.fold_in(key, 11), 3)
    lists = N_REP * N_DOM
    lowest = max(TILES // 2, 1)
    spread = jax.random.randint(keys[0], (lists,), lowest, TILES + 1)
    chosen = jax.random.randint(keys[1], (), 0, lists)
    second = (chosen + 1 + jax.random.randint(keys[2], (), 0, lists - 1)) % lists
    positions = jnp.arange(lists)
    filled = jnp.where(positions == chosen, TILES, jnp.where(positions == second, lowest, spread))
    return filled.reshape(N_REP, N_DOM).astype(jnp.int32)


def shard_levels(own_key, extent, pieces, low, top_value):
    def one(axis_at, blocks):
        heights = jax.random.uniform(jax.random.fold_in(jax.random.fold_in(own_key, 6), axis_at), (blocks,), jnp.float32, low / len(pieces), top_value / len(pieces))
        return jnp.repeat(jnp.exp(heights), extent[axis_at] // blocks).reshape((-1,) + (1,) * (len(extent) - axis_at - 1))

    gain = one(*pieces[0])
    for cut in pieces[1:]:
        gain = gain * one(*cut)
    return gain


def gaussian(own_key, extent, scale, reach, cuts=(), kind=jnp.bfloat16):
    gain = shard_levels(own_key, extent, cuts, -0.22, 0.18) if cuts else 1.0
    result = jax.random.normal(own_key, extent, jnp.float32) * scale * gain
    return jnp.minimum(jnp.maximum(result, -reach), reach).astype(kind)


def setup_inputs(seed: int = 0) -> dict:
    key_list = jax.random.split(jax.random.key(seed), 9)
    return {
        "feats": gaussian(key_list[0], (NODES, HID), 1.0, 6.0, ((0, 512),)),
        "w_self": gaussian(key_list[1], (HID, HID), HID ** -0.5, 0.375),
        "w_neigh": gaussian(key_list[2], (HID, HID), (HID // 16) ** -0.5, 1.5),
        "tile_vals": jnp.clip(1.0 * jax.random.uniform(key_list[3], (N_REP, N_DOM, TILES, TILE, TILE), jnp.float32) ** shard_levels(key_list[3], (N_REP, N_DOM, TILES, TILE, TILE), ((0, 8), (1, 64)), -0.2, 0.2), 0.0, 1.0).astype(jnp.bfloat16),
        "tile_owner": draw_tile_owner(jax.random.fold_in(key_list[8], 71), 0),
        "tile_src": draw_tile_src(jax.random.fold_in(key_list[8], 71), 0),
        "tile_count": draw_tile_count(jax.random.fold_in(key_list[8], 71), 0),
        "d_out": gaussian(key_list[7], (NODES, HID), 1.0, 6.0, ((0, 512),)),
    }


def reference(feats, w_self, w_neigh, tile_vals, tile_owner, tile_src, tile_count, d_out):
    per_block = ROWS // TILE
    hidden = feats.shape[1]
    lists = N_REP * N_DOM
    flat_vals = tile_vals.reshape(lists, TILES, TILE, TILE)
    flat_owner = tile_owner.reshape(lists, TILES)
    flat_src = tile_src.reshape(lists, TILES)
    flat_count = tile_count.reshape(lists)
    list_ids = jnp.arange(lists, dtype=jnp.int32)
    feat_tiles = feats.reshape(NODES // TILE, TILE, hidden)

    def placement(list_id, owners, sources, live_count):
        rep_id = list_id // N_DOM
        dom_id = list_id % N_DOM
        dest_rows = (rep_id * (N_DOM * per_block) + owners).astype(jnp.int32)
        src_rows = (((sources // per_block) * N_DOM + dom_id) * per_block + sources % per_block).astype(jnp.int32)
        live_mask = (jnp.arange(TILES, dtype=jnp.int32) < live_count).astype(jnp.float32)
        return dest_rows, src_rows, live_mask

    def forward_list(state_pair, inputs):
        neigh_sum, degree_sum = state_pair
        list_id, tile_block, owners, sources, live_count = inputs
        dest_rows, src_rows, live_mask = placement(list_id, owners, sources, live_count)
        block_f = tile_block.astype(jnp.float32)
        product = jnp.einsum("tij,tjc->tic", block_f, feat_tiles[src_rows].astype(jnp.float32), precision=lax.Precision.HIGHEST)
        neigh_sum = neigh_sum.at[dest_rows].add(product * live_mask[:, None, None])
        degree_sum = degree_sum.at[dest_rows].add(jnp.sum(block_f, axis=2) * live_mask[:, None])
        return (neigh_sum, degree_sum), None

    start_sum = jnp.zeros((NODES // TILE, TILE, hidden), jnp.float32)
    start_deg = jnp.zeros((NODES // TILE, TILE), jnp.float32)
    (neigh_sum, degree_sum), _ = lax.scan(forward_list, (start_sum, start_deg), (list_ids, flat_vals, flat_owner, flat_src, flat_count))
    degree = 1.0 + degree_sum.reshape(NODES)
    mean_agg = (neigh_sum.reshape(NODES, hidden) / degree[:, None]).astype(jnp.bfloat16)
    pre_act = jnp.dot(feats, w_self, preferred_element_type=jnp.float32) + jnp.dot(mean_agg, w_neigh, preferred_element_type=jnp.float32)
    sigmoid_pre = jax.nn.sigmoid(pre_act)
    out_feats = (pre_act * sigmoid_pre).astype(jnp.bfloat16)
    d_pre = (d_out.astype(jnp.float32) * sigmoid_pre * (1.0 + pre_act * (1.0 - sigmoid_pre))).astype(jnp.bfloat16)
    grad_self = jnp.dot(feats.T, d_pre, preferred_element_type=jnp.float32)
    grad_neigh = jnp.dot(mean_agg.T, d_pre, preferred_element_type=jnp.float32)
    d_sum = (jnp.dot(d_pre, w_neigh.T, preferred_element_type=jnp.float32) / degree[:, None]).astype(jnp.bfloat16)
    d_sum_tiles = d_sum.reshape(NODES // TILE, TILE, hidden)

    def backward_list(grad_tiles, inputs):
        list_id, tile_block, owners, sources, live_count = inputs
        dest_rows, src_rows, live_mask = placement(list_id, owners, sources, live_count)
        contrib = jnp.einsum("tij,tic->tjc", tile_block.astype(jnp.float32), d_sum_tiles[dest_rows].astype(jnp.float32), precision=lax.Precision.HIGHEST)
        return grad_tiles.at[src_rows].add(contrib * live_mask[:, None, None]), None

    grad_tiles, _ = lax.scan(backward_list, jnp.zeros((NODES // TILE, TILE, hidden), jnp.float32), (list_ids, flat_vals, flat_owner, flat_src, flat_count))
    d_feats = (jnp.dot(d_pre, w_self.T, preferred_element_type=jnp.float32) + grad_tiles.reshape(NODES, hidden)).astype(jnp.bfloat16)
    return (out_feats, d_feats, grad_self, grad_neigh)
```

```python
import jax
import jax.numpy as jnp
from jax import lax
from jax.experimental import pallas as pl
from jax.experimental.pallas import tpu as pltpu
from jax.sharding import Mesh
from jax.sharding import PartitionSpec as P


BF = jnp.bfloat16
F32 = jnp.float32
NX, NZ, NC, NR = 4, 8, 2, 8
T = 128
H = 256
CHUNK = 16
DEG = 8
GRAD = 8
BLK = H + 2 * DEG
VMEM = pl.BlockSpec(memory_space=pltpu.VMEM)
SMEM = pl.BlockSpec(memory_space=pltpu.SMEM)
ANY = pl.BlockSpec(memory_space=pl.ANY)
PARAMS = pltpu.CompilerParams(vmem_limit_bytes=56 * 1024 * 1024)
NT = (((1,), (1,)), ((), ()))
TN = (((0,), (0,)), ((), ()))


def dot(a, b, dims=(((1,), (0,)), ((), ()))):
    return lax.dot_general(a, b, dims, preferred_element_type=F32)


def split_degree(deg):
    high = deg.astype(BF).astype(F32)
    return jnp.concatenate([high, deg - high], axis=0).astype(BF)


def add_blocks(blocks):
    total = blocks[0].astype(F32)
    for block in blocks[1:]:
        total = total + block.astype(F32)
    return total[:H], total[H : H + DEG] + total[H + DEG :]


def tile_copy(vals, tiles, sems, chunk):
    part = pl.ds(chunk * CHUNK, CHUNK)
    return pltpu.make_async_copy(vals.at[part], tiles.at[part], sems.at[chunk])


def over_live_tiles(vals, tiles, sems, count, prepare, one_tile):
    n_chunks = tiles.shape[0] // CHUNK
    for chunk in range(n_chunks):

        @pl.when(chunk * CHUNK < count)
        def _():
            tile_copy(vals, tiles, sems, chunk).start()

    prepare()

    @pl.loop(0, n_chunks)
    def _(chunk):
        @pl.when(chunk * CHUNK < count)
        def _():
            tile_copy(vals, tiles, sems, chunk).wait()
            first = chunk * CHUNK
            live = jnp.minimum(count - first, CHUNK)

            @pl.loop(0, live // 4)
            def _(quad):
                one_tile([first + quad * 4 + k for k in range(4)])

            @pl.loop(live // 4 * 4, live)
            def _(t):
                one_tile([first + t])


def forward_kernel(owners, sources, meta, vals, panel, keep, send, tiles, acc, lhs, sems):
    count, my_x, my_core = meta[0], meta[1], meta[2]

    def prepare():
        acc[...] = jnp.zeros(acc.shape, F32)
        for s in range(NR):
            lhs[s, :H] = panel[s].astype(F32).T.astype(BF)
            lhs[s, H:] = jnp.ones((2 * DEG, T), BF)

    def one_tile(ts):
        prods = [dot(lhs[sources[t]], tiles[t], NT) for t in ts]
        for t, prod in zip(ts, prods):
            owner = owners[t]
            slot = ((owner & 1) ^ my_core) * (NX * NZ) + (((owner >> 4) - my_x) & 3) * NZ
            slot = slot + ((owner >> 1) & 7)
            acc[slot] = acc[slot] + prod[: H + DEG]

    over_live_tiles(vals, tiles, sems, count, prepare, one_tile)

    @pl.loop(0, NX * NZ)
    def _(b):
        for half, out in enumerate((keep, send)):
            out[b, :H] = acc[half * NX * NZ + b, :H].astype(BF)
            out[b, H:] = split_degree(acc[half * NX * NZ + b, H:])


def forward(owners, sources, meta, vals, panel):
    n = vals.shape[0]
    half = jax.ShapeDtypeStruct((NX * NZ, BLK, T), BF)
    return pl.pallas_call(
        forward_kernel,
        in_specs=[SMEM, SMEM, SMEM, ANY, VMEM],
        out_specs=(VMEM, VMEM),
        out_shape=(half, half),
        scratch_shapes=[
            pltpu.VMEM((n, T, T), BF),
            pltpu.VMEM((NC * NX * NZ, H + DEG, T), F32),
            pltpu.VMEM((NR, BLK, T), BF),
            pltpu.SemaphoreType.DMA((n // CHUNK,)),
        ],
        compiler_params=PARAMS,
        name="forward_tiles",
    )(owners, sources, meta, vals, panel)


def core_sum_kernel(a, b, *outs):
    @pl.loop(0, NZ)
    def _(z):
        for k, out in enumerate(outs):
            sums, deg = add_blocks([a[k * NZ + z], b[k * NZ + z]])
            out[z, :H] = sums.astype(BF)
            out[z, H:] = split_degree(deg)


def core_sum(a, b):
    part = jax.ShapeDtypeStruct((NZ, BLK, T), BF)
    return pl.pallas_call(
        core_sum_kernel,
        in_specs=[VMEM, VMEM],
        out_specs=(VMEM,) * NX,
        out_shape=(part,) * NX,
        compiler_params=PARAMS,
        name="core_sum",
    )(a, b)


def x_sum_kernel(*refs):
    *parts, out = refs

    @pl.loop(0, NZ)
    def _(z):
        sums, deg = add_blocks([p[z] for p in parts])
        out[z, :H] = sums.astype(BF)
        out[z, H:] = split_degree(deg)


def x_sum(parts):
    return pl.pallas_call(
        x_sum_kernel,
        in_specs=[VMEM] * NX,
        out_specs=VMEM,
        out_shape=jax.ShapeDtypeStruct((NZ, BLK, T), BF),
        compiler_params=PARAMS,
        name="x_sum",
    )(*parts)


def node_kernel(parts, feats, d_out, w_self, w_neigh, out_feats, d_sum, base, grads):
    sums, deg = add_blocks([parts[z] for z in range(NZ)])
    deg = 1.0 + deg[:1]
    mean_t = (sums / deg).astype(BF)
    pre = dot(feats[...], w_self[...]) + dot(mean_t, w_neigh[...], TN)
    gate = jax.nn.sigmoid(pre)
    out_feats[...] = (pre * gate).astype(BF)
    d_pre = (d_out[...].astype(F32) * gate * (1.0 + pre * (1.0 - gate))).astype(BF)
    d_sum[...] = (dot(w_neigh[...], d_pre, NT) / deg).astype(BF)
    base[...] = dot(w_self[...], d_pre, NT)
    rows = GRAD // 2
    for part, grad in enumerate((dot(feats[...], d_pre, TN), dot(mean_t, d_pre))):
        for g in range(H // rows):
            grads[g, part * rows : (part + 1) * rows] = grad[g * rows : (g + 1) * rows]


def node(parts, feats, d_out, w_self, w_neigh):
    return pl.pallas_call(
        node_kernel,
        in_specs=[VMEM] * 5,
        out_specs=(VMEM,) * 4,
        out_shape=(
            jax.ShapeDtypeStruct((T, H), BF),
            jax.ShapeDtypeStruct((H, T), BF),
            jax.ShapeDtypeStruct((H, T), F32),
            jax.ShapeDtypeStruct((NX * NZ * NC, GRAD, H), F32),
        ),
        compiler_params=PARAMS,
        name="node",
    )(parts, feats, d_out, w_self, w_neigh)


def backward_kernel(owners, sources, meta, vals, *refs):
    pieces, (grads, out, tiles, acc, lhs, sems, piece_sems) = refs[: NC * NX], refs[NC * NX :]
    count, my_x, my_core = meta[0], meta[1], meta[2]

    def piece_copy(k):
        return pltpu.make_async_copy(pieces[k], lhs.at[pl.ds(k * NZ, NZ)], piece_sems.at[k])

    def prepare():
        for k in range(NC * NX):
            piece_copy(k).start()
        acc[...] = jnp.zeros(acc.shape, F32)
        for k in range(NC * NX):
            piece_copy(k).wait()

    def one_tile(ts):
        prods = []
        for t in ts:
            owner = owners[t]
            slot = ((owner & 1) ^ my_core) * (NX * NZ) + ((my_x - (owner >> 4)) & 3) * NZ
            prods.append(dot(lhs[slot + ((owner >> 1) & 7)], tiles[t]))
        for t, prod in zip(ts, prods):
            acc[sources[t]] = acc[sources[t]] + prod

    over_live_tiles(vals, tiles, sems, count, prepare, one_tile)
    grad = jnp.sum(grads[...], axis=0)
    high = grad.astype(BF).astype(F32)
    parts = [p[:, k : k + T] for p in (high, grad - high) for k in range(0, H, T)]
    grad_rows = jnp.concatenate(parts, axis=0).astype(BF)
    for s in range(NR):
        out[s, :H] = acc[s].astype(BF)
        out[s, H:] = grad_rows


def backward(owners, sources, meta, vals, pieces, grads):
    n = vals.shape[0]
    return pl.pallas_call(
        backward_kernel,
        in_specs=[SMEM, SMEM, SMEM, ANY] + [ANY] * (NC * NX) + [VMEM],
        out_specs=VMEM,
        out_shape=jax.ShapeDtypeStruct((NR, H + 4 * GRAD, T), BF),
        scratch_shapes=[
            pltpu.VMEM((n, T, T), BF),
            pltpu.VMEM((NR, H, T), F32),
            pltpu.VMEM((NC * NX * NZ, H, T), BF),
            pltpu.SemaphoreType.DMA((n // CHUNK,)),
            pltpu.SemaphoreType.DMA((NC * NX,)),
        ],
        compiler_params=PARAMS,
        name="backward_tiles",
    )(owners, sources, meta, vals, *pieces, grads)


def final_kernel(parts, base, out, grads):
    total = parts[0].astype(F32)
    for r in range(1, NR):
        total = total + parts[r].astype(F32)
    out[...] = (base[...] + total[:H]).T.astype(BF)
    for k in range(H // T):
        high, low = (total[H + (2 * p + k) * GRAD :][:GRAD] for p in range(2))
        grads[:, k * T : (k + 1) * T] = high + low


def final(parts, base):
    return pl.pallas_call(
        final_kernel,
        in_specs=[VMEM, VMEM],
        out_specs=(VMEM, VMEM),
        out_shape=(jax.ShapeDtypeStruct((T, H), BF), jax.ShapeDtypeStruct((GRAD, H), F32)),
        compiler_params=PARAMS,
        name="final",
    )(parts, base)


def shift(size, by):
    return [(i, (i + by) % size) for i in range(size)]


def per_device(feats, w_self, w_neigh, tile_vals, tile_owner, tile_src, tile_count, d_out):
    owners, sources, vals = tile_owner[0, 0], tile_src[0, 0], tile_vals[0, 0]
    meta = jnp.stack([tile_count[0, 0], lax.axis_index("x"), lax.axis_index("core")])
    swap = shift(NC, 1)

    panel = lax.all_gather(feats, "rep", axis=0)
    keep, send = forward(owners, sources, meta, vals, panel)
    parts = core_sum(keep, lax.ppermute(send, "core", swap))
    parts = [parts[0]] + [lax.ppermute(parts[k], "x", shift(NX, k)) for k in range(1, NX)]
    mine = lax.all_to_all(x_sum(parts), "z", 0, 0)

    out_feats, d_sum, base, grads = node(mine, feats, d_out, w_self, w_neigh)

    grads = lax.all_to_all(grads, ("x", "z", "core"), 0, 0)
    near = lax.all_gather(d_sum, "z", axis=0)
    pieces = [near] + [lax.ppermute(near, "x", shift(NX, k)) for k in range(1, NX)]
    pieces = pieces + [lax.ppermute(p, "core", swap) for p in pieces]
    back = backward(owners, sources, meta, vals, pieces, grads)
    d_feats, grads = final(lax.all_to_all(back, "rep", 0, 0), base)
    return out_feats, d_feats, grads[: GRAD // 2], grads[GRAD // 2 :]


def solution(mesh):
    split = Mesh(mesh.devices.reshape(NR, NX, NZ, NC), ("rep", "x", "z", "core"))
    dom = ("x", "z", "core")
    nodes = P(("rep", *dom), None)
    in_specs = (
        nodes,
        P(),
        P(),
        P("rep", dom, None, None, None),
        P("rep", dom, None),
        P("rep", dom, None),
        P("rep", dom),
        nodes,
    )
    out_specs = (nodes, nodes, P(dom, None), P(dom, None))
    return jax.shard_map(
        per_device, mesh=split, in_specs=in_specs, out_specs=out_specs, check_vma=False
    )
```

```python
import jax
import jax.numpy as jnp
from jax import lax
from jax.experimental import pallas as pl
from jax.experimental.pallas import tpu as pltpu
from jax.sharding import Mesh
from jax.sharding import PartitionSpec as P


BF = jnp.bfloat16
F32 = jnp.float32
NX, NZ, NC, NR = 4, 8, 2, 8
T = 128
H = 256
HALF = NX * NZ
DEG = 8
GRAD = 8
BLK = H + 2 * DEG
VMEM = pl.BlockSpec(memory_space=pltpu.VMEM)
SMEM = pl.BlockSpec(memory_space=pltpu.SMEM)
PARAMS = pltpu.CompilerParams(vmem_limit_bytes=20 * 1024 * 1024)
NT = (((1,), (1,)), ((), ()))
TN = (((0,), (0,)), ((), ()))


def dot(a, b, dims=(((1,), (0,)), ((), ()))):
    return lax.dot_general(a, b, dims, preferred_element_type=F32)


def call(kernel, name, out_shape, *args, scratch=(), cost=None):
    spec = lambda a: SMEM if a.dtype == jnp.int32 else VMEM
    args = [a if a.dtype == jnp.int32 else pltpu.with_memory_space_constraint(a, pltpu.VMEM) for a in args]
    return pl.pallas_call(
        kernel,
        in_specs=[spec(a) for a in args],
        out_specs=jax.tree.map(spec, out_shape, is_leaf=lambda a: hasattr(a, "dtype")),
        out_shape=out_shape,
        scratch_shapes=scratch,
        compiler_params=PARAMS,
        cost_estimate=cost,
        name=name,
    )(*args)


def split_degree(deg):
    high = deg.astype(BF).astype(F32)
    return jnp.concatenate([high, deg - high], axis=0).astype(BF)


def add_blocks(blocks):
    sums, deg = 0.0, 0.0
    for block in blocks:
        block = block.astype(F32)
        sums = sums + block[:H]
        deg = deg + block[H : H + DEG]
        if block.shape[0] == BLK:
            deg = deg + block[H + DEG :]
    return sums, deg


def spread_kernel(feats, out):
    block = feats[...].astype(F32).T.astype(BF)
    for r in range(NR):
        out[r] = block


def spread(feats):
    return call(spread_kernel, "spread", pltpu.VMEM((NR, H, T), BF), feats)


def order_kernel(owners, sources, meta, ids, slots, srcs, counts):
    n = owners.shape[0]

    def step(t, placed):
        owner = owners[t]
        far = (owner & 1) ^ meta[2]
        at = far * n + jnp.where(far == 1, placed[1], placed[0])
        ids[at] = t
        slots[at] = (((owner >> 4) - meta[1]) & (NX - 1)) * NZ + ((owner >> 1) & (NZ - 1))
        srcs[at] = sources[t]
        return placed[0] + 1 - far, placed[1] + far

    counts[0], counts[1] = lax.fori_loop(0, meta[0], step, (jnp.int32(0), jnp.int32(0)))


def order(owners, sources, meta):
    lists = jax.ShapeDtypeStruct((2 * owners.shape[0],), jnp.int32)
    out_shape = (lists, lists, lists, jax.ShapeDtypeStruct((2,), jnp.int32))
    return call(order_kernel, "order", out_shape, owners, sources, meta)


def over_tiles(first, count, step):
    @pl.loop(0, count // 4)
    def _(quad):
        step([first + quad * 4 + k for k in range(4)])

    @pl.loop(count // 4 * 4, count)
    def _(k):
        step([first + k])


def forward_sums(far, ids, slots, srcs, counts, tiles, panel, acc, lhs):
    acc[...] = jnp.zeros(acc.shape, F32)
    for s in range(NR):
        lhs[s, :H] = panel[s]
        lhs[s, H:] = jnp.ones((2 * DEG, T), BF)

    def step(ns):
        prods = [dot(lhs[srcs[n]], tiles[ids[n]], NT) for n in ns]
        for n, prod in zip(ns, prods):
            acc[slots[n]] = acc[slots[n]] + prod[: H + DEG]

    over_tiles(far * tiles.shape[0], counts[far], step)


def forward_far_kernel(ids, slots, srcs, counts, tiles, panel, out, acc, lhs):
    forward_sums(1, ids, slots, srcs, counts, tiles, panel, acc, lhs)

    @pl.loop(0, HALF)
    def _(b):
        out[b, :H] = acc[b, :H].astype(BF)
        out[b, H:] = split_degree(acc[b, H:])


def forward_near_kernel(ids, slots, srcs, counts, tiles, panel, out, lhs):
    forward_sums(0, ids, slots, srcs, counts, tiles, panel, out, lhs)


FORWARD_COST = pl.CostEstimate(flops=64 * 2 * BLK * T * T, bytes_accessed=2**21, transcendentals=0)
BACKWARD_COST = FORWARD_COST


def forward_far(lists, tiles, panel):
    scratch = [pltpu.VMEM((HALF, H + DEG, T), F32), pltpu.VMEM((NR, BLK, T), BF)]
    out_shape = pltpu.VMEM((HALF, BLK, T), BF)
    return call(forward_far_kernel, "forward_far", out_shape, *lists, tiles, panel, scratch=scratch, cost=FORWARD_COST)


def forward_near(lists, tiles, panel):
    scratch = [pltpu.VMEM((NR, BLK, T), BF)]
    out_shape = pltpu.VMEM((HALF, H + DEG, T), F32)
    return call(forward_near_kernel, "forward_near", out_shape, *lists, tiles, panel, scratch=scratch, cost=FORWARD_COST)


def core_sum(near, other, dx):
    def kernel(a, b, out):
        @pl.loop(0, NZ)
        def _(z):
            sums, deg = add_blocks([a[dx * NZ + z], b[dx * NZ + z]])
            out[z, :H] = sums.astype(BF)
            out[z, H:] = split_degree(deg)

    return call(kernel, f"core_sum_{dx}", pltpu.VMEM((NZ, BLK, T), BF), near, other)


def x_sum_kernel(near, other, *refs):
    *parts, out = refs

    @pl.loop(0, NZ)
    def _(z):
        sums, deg = add_blocks([p[z] for p in (near, other, *parts)])
        out[z, :H] = sums.astype(BF)
        out[z, H:] = split_degree(deg)


def x_sum(near, other, parts):
    return call(x_sum_kernel, "x_sum", pltpu.VMEM((NZ, BLK, T), BF), near, other, *parts)


def node_kernel(parts, feats, d_out, w_self, w_neigh, out_feats, d_sum, base, grads):
    sums, deg = add_blocks([parts[z] for z in range(NZ)])
    deg = 1.0 + deg[:1]
    mean_t = (sums / deg).astype(BF)
    pre = dot(feats[...], w_self[...]) + dot(mean_t, w_neigh[...], TN)
    gate = jax.nn.sigmoid(pre)
    out_feats[...] = (pre * gate).astype(BF)
    d_pre = (d_out[...].astype(F32) * gate * (1.0 + pre * (1.0 - gate))).astype(BF)
    d_sum_t = (dot(w_neigh[...], d_pre, NT) / deg).astype(BF)
    for z in range(NZ):
        d_sum[z] = d_sum_t
    base[...] = dot(w_self[...], d_pre, NT)
    rows = GRAD // 2
    for part, grad in enumerate((dot(feats[...], d_pre, TN), dot(mean_t, d_pre))):
        for g in range(H // rows):
            grads[g, part * rows : (part + 1) * rows] = grad[g * rows : (g + 1) * rows]


def node(parts, feats, d_out, w_self, w_neigh):
    out_shape = (
        jax.ShapeDtypeStruct((T, H), BF),
        pltpu.VMEM((NZ, H, T), BF),
        pltpu.VMEM((H, T), F32),
        pltpu.VMEM((NX * NZ * NC, GRAD, H), F32),
    )
    return call(node_kernel, "node", out_shape, parts, feats, d_out, w_self, w_neigh)


def backward_sums(far, ids, slots, srcs, counts, tiles, pieces, acc, lhs):
    for k in range(NX):
        lhs[k * NZ : (k + 1) * NZ] = pieces[k][...]

    def step(ns):
        prods = []
        for n in ns:
            back = (-(slots[n] >> 3) & (NX - 1)) * NZ + (slots[n] & (NZ - 1))
            prods.append(dot(lhs[back], tiles[ids[n]]))
        for n, prod in zip(ns, prods):
            acc[srcs[n]] = acc[srcs[n]] + prod

    over_tiles(far * tiles.shape[0], counts[far], step)


def backward_near_kernel(ids, slots, srcs, counts, tiles, *refs):
    *pieces, out, lhs = refs
    out[...] = jnp.zeros(out.shape, F32)
    backward_sums(0, ids, slots, srcs, counts, tiles, pieces, out, lhs)


def backward_far_kernel(ids, slots, srcs, counts, tiles, *refs):
    *pieces, near, grads, out, acc, lhs = refs
    acc[...] = near[...]
    backward_sums(1, ids, slots, srcs, counts, tiles, pieces, acc, lhs)
    grad = jnp.sum(grads[...], axis=0)
    high = grad.astype(BF).astype(F32)
    parts = [p[:, k : k + T] for p in (high, grad - high) for k in range(0, H, T)]
    grad_rows = jnp.concatenate(parts, axis=0).astype(BF)
    for s in range(NR):
        out[s, :H] = acc[s].astype(BF)
        out[s, H:] = grad_rows


def backward_near(lists, tiles, pieces):
    scratch = [pltpu.VMEM((HALF, H, T), BF)]
    out_shape = pltpu.VMEM((NR, H, T), F32)
    return call(backward_near_kernel, "backward_near", out_shape, *lists, tiles, *pieces, scratch=scratch, cost=BACKWARD_COST)


def backward_far(lists, tiles, pieces, near, grads):
    scratch = [pltpu.VMEM((NR, H, T), F32), pltpu.VMEM((HALF, H, T), BF)]
    out_shape = pltpu.VMEM((NR, H + 4 * GRAD, T), BF)
    args = (*lists, tiles, *pieces, near, grads)
    return call(backward_far_kernel, "backward_far", out_shape, *args, scratch=scratch, cost=BACKWARD_COST)


def final_kernel(parts, base, out, *grads):
    total = parts[0].astype(F32)
    for r in range(1, NR):
        total = total + parts[r].astype(F32)
    out[...] = (base[...] + total[:H]).T.astype(BF)
    rows = GRAD // 2
    for k in range(H // T):
        high, low = (total[H + (2 * p + k) * GRAD :][:GRAD] for p in range(2))
        for part, grad in enumerate(grads):
            grad[:, k * T : (k + 1) * T] = (high + low)[part * rows : (part + 1) * rows]


def final(parts, base):
    grad = jax.ShapeDtypeStruct((GRAD // 2, H), F32)
    return call(final_kernel, "final", (jax.ShapeDtypeStruct((T, H), BF), grad, grad), parts, base)


def shift(size, by):
    return [(i, (i + by) % size) for i in range(size)]


def per_device(feats, w_self, w_neigh, tile_vals, tile_owner, tile_src, tile_count, d_out):
    tiles = pltpu.with_memory_space_constraint(tile_vals[0, 0], pltpu.VMEM)
    meta = jnp.stack([tile_count[0, 0], lax.axis_index("x"), lax.axis_index("core")])
    swap = shift(NC, 1)

    panel = lax.all_to_all(spread(feats), "rep", 0, 0)
    lists = order(tile_owner[0, 0], tile_src[0, 0], meta)
    far = forward_far(lists, tiles, panel)
    near = forward_near(lists, tiles, panel)
    other = lax.ppermute(far, "core", swap)
    parts = [lax.ppermute(core_sum(near, other, k), "x", shift(NX, k)) for k in range(1, NX)]
    mine = lax.all_to_all(x_sum(near, other, parts), "z", 0, 0)

    out_feats, d_sum, base, grads = node(mine, feats, d_out, w_self, w_neigh)

    grads = lax.all_to_all(grads, ("x", "z", "core"), 0, 0)
    column = lax.all_to_all(d_sum, "z", 0, 0)
    pieces = [column] + [lax.ppermute(column, "x", shift(NX, k)) for k in range(1, NX)]
    others = [lax.ppermute(p, "core", swap) for p in pieces]
    back = backward_near(lists, tiles, pieces)
    back = backward_far(lists, tiles, others, back, grads)
    return (out_feats, *final(lax.all_to_all(back, "rep", 0, 0), base))


def solution(mesh):
    split = Mesh(mesh.devices.reshape(NR, NX, NZ, NC), ("rep", "x", "z", "core"))
    dom = ("x", "z", "core")
    nodes = P(("rep", *dom), None)
    in_specs = (
        nodes,
        P(),
        P(),
        P("rep", dom, None, None, None),
        P("rep", dom, None),
        P("rep", dom, None),
        P("rep", dom),
        nodes,
    )
    out_specs = (nodes, nodes, P(dom, None), P(dom, None))
    return jax.shard_map(
        per_device, mesh=split, in_specs=in_specs, out_specs=out_specs, check_vma=False
    )
```

```python
import jax
import jax.numpy as jnp
from jax import lax
from jax.experimental import pallas as pl
from jax.experimental.pallas import tpu as pltpu
from jax.sharding import Mesh
from jax.sharding import PartitionSpec as P


BF = jnp.bfloat16
F32 = jnp.float32
NX, NZ, NC, NR = 4, 8, 2, 8
T = 128
H = 256
TILES = 128
SLOTS = 144
HALF = NX * NZ
DEG = 8
GRAD = 8
BLK = H + 2 * DEG
VMEM = pl.BlockSpec(memory_space=pltpu.VMEM)
SMEM = pl.BlockSpec(memory_space=pltpu.SMEM)
HBM = pl.BlockSpec(memory_space=pltpu.HBM)
PARAMS = pltpu.CompilerParams(vmem_limit_bytes=20 * 1024 * 1024)
NT = (((1,), (1,)), ((), ()))
TN = (((0,), (0,)), ((), ()))


def dot(a, b, dims=(((1,), (0,)), ((), ()))):
    return lax.dot_general(a, b, dims, preferred_element_type=F32)


def call(kernel, out_shape, *args, scratch=(), cost=None):
    def spec(a):
        return SMEM if a.dtype == jnp.int32 else HBM if a.shape == (TILES, T, T) else VMEM

    def place(a):
        s = spec(a)
        return a if s is SMEM else pltpu.with_memory_space_constraint(a, s.memory_space)

    args = [place(a) for a in args]
    return pl.pallas_call(
        kernel,
        in_specs=[spec(a) for a in args],
        out_specs=jax.tree.map(spec, out_shape, is_leaf=lambda a: hasattr(a, "dtype")),
        out_shape=out_shape,
        scratch_shapes=scratch,
        compiler_params=PARAMS,
        cost_estimate=cost,
    )(*args)


def split_degree(deg):
    high = deg.astype(BF).astype(F32)
    return jnp.concatenate([high, deg - high], axis=0).astype(BF)


def add_blocks(blocks):
    sums, deg = 0.0, 0.0
    for block in blocks:
        block = block.astype(F32)
        sums = sums + block[:H]
        deg = deg + block[H : H + DEG]
        if block.shape[0] == BLK:
            deg = deg + block[H + DEG :]
    return sums, deg


def spread_kernel(feats, out):
    block = feats[...].astype(F32).T.astype(BF)
    for r in range(NR):
        out[r] = block


def spread(feats):
    return call(spread_kernel, pltpu.VMEM((NR, H, T), BF), feats)


def order_kernel(owners, sources, meta, ids, owner_slots, srcs, pairs, seen):
    count, my_core = meta[0], meta[2]

    def bucket(t):
        return ((owners[t] & 1) ^ my_core) * NR + sources[t]

    @pl.loop(0, NC * NR)
    def _(b):
        seen[b] = 0

    @pl.loop(0, count)
    def _(t):
        seen[bucket(t)] = seen[bucket(t)] + 1

    for far in range(NC):
        at = jnp.int32(far * SLOTS)
        for src in range(NR):
            size = seen[far * NR + src]
            seen[far * NR + src] = at
            at = at + size

            @pl.when(size % 2 == 1)
            def _():
                ids[at], owner_slots[at], srcs[at] = -1, 0, src

            at = at + size % 2
        pairs[far] = (at - far * SLOTS) // 2

    @pl.loop(0, count)
    def _(t):
        at = seen[bucket(t)]
        seen[bucket(t)] = at + 1
        ids[at] = t
        owner_slots[at] = owners[t] >> 1
        srcs[at] = sources[t]


def order(owners, sources, meta):
    lists = jax.ShapeDtypeStruct((NC * SLOTS,), jnp.int32)
    out_shape = (lists, lists, lists, jax.ShapeDtypeStruct((NC,), jnp.int32))
    scratch = [pltpu.SMEM((NC * NR,), jnp.int32)]
    return call(order_kernel, out_shape, owners, sources, meta, scratch=scratch)


def over_pairs(far, ids, pairs, vals, buffers, prepare, step):
    tiles, sems = buffers
    first, n_pairs = far * SLOTS, pairs[far]

    def copy(k):
        return pltpu.make_async_copy(vals.at[ids[first + k]], tiles.at[k], sems.at[k])

    @pl.loop(0, n_pairs * 2)
    def _(k):
        real = ids[first + k] >= 0

        @pl.when(real)
        def _():
            copy(k).start()

        @pl.when(jnp.logical_not(real))
        def _():
            tiles[k] = jnp.zeros((T, T), BF)

    prepare()

    def run(ps):
        for p in ps:
            copy(p * 2).wait()

            @pl.when(ids[first + p * 2 + 1] >= 0)
            def _():
                copy(p * 2 + 1).wait()

        step([(first + p * 2, tiles[pl.ds(p * 2, 2)].reshape(2 * T, T)) for p in ps])

    @pl.loop(0, n_pairs // 2)
    def _(q):
        run([q * 2, q * 2 + 1])

    @pl.when(n_pairs % 2 == 1)
    def _():
        run([n_pairs - 1])


def forward_sums(far, ids, slots, srcs, pairs, my_x, vals, panel, acc, lhs, buffers):
    def prepare():
        acc[...] = jnp.zeros(acc.shape, F32)
        for s in range(NR):
            lhs[s, :H] = panel[s]
            lhs[s, H:] = jnp.ones((2 * DEG, T), BF)

    def step(tiles):
        prods = [dot(lhs[srcs[n]], pair, NT) for n, pair in tiles]
        for (n, _), prod in zip(tiles, prods):
            for k in range(2):
                slot = (slots[n + k] - my_x[0] * NZ) & (HALF - 1)
                acc[slot] = acc[slot] + prod[: H + DEG, k * T : (k + 1) * T]

    over_pairs(far, ids, pairs, vals, buffers, prepare, step)


def forward_far_kernel(ids, slots, srcs, pairs, my_x, vals, panel, out, acc, lhs, *buffers):
    forward_sums(1, ids, slots, srcs, pairs, my_x, vals, panel, acc, lhs, buffers)

    @pl.loop(0, HALF)
    def _(b):
        out[b, :H] = acc[b, :H].astype(BF)
        out[b, H:] = split_degree(acc[b, H:])


def forward_near_kernel(ids, slots, srcs, pairs, my_x, vals, panel, out, lhs, *buffers):
    forward_sums(0, ids, slots, srcs, pairs, my_x, vals, panel, out, lhs, buffers)


FORWARD_COST = pl.CostEstimate(flops=64 * 2 * BLK * T * T, bytes_accessed=2**21, transcendentals=0)
BACKWARD_COST = FORWARD_COST
BUFFERS = [pltpu.VMEM((SLOTS, T, T), BF), pltpu.SemaphoreType.DMA((SLOTS,))]


def forward_far(lists, my_x, tiles, panel):
    scratch = [pltpu.VMEM((HALF, H + DEG, T), F32), pltpu.VMEM((NR, BLK, T), BF), *BUFFERS]
    out_shape = pltpu.VMEM((HALF, BLK, T), BF)
    return call(forward_far_kernel, out_shape, *lists, my_x, tiles, panel, scratch=scratch, cost=FORWARD_COST)


def forward_near(lists, my_x, tiles, panel):
    scratch = [pltpu.VMEM((NR, BLK, T), BF), *BUFFERS]
    out_shape = pltpu.VMEM((HALF, H + DEG, T), F32)
    return call(forward_near_kernel, out_shape, *lists, my_x, tiles, panel, scratch=scratch, cost=FORWARD_COST)


def core_sum(near, other, dx):
    def kernel(a, b, out):
        @pl.loop(0, NZ)
        def _(z):
            sums, deg = add_blocks([a[dx * NZ + z], b[dx * NZ + z]])
            out[z, :H] = sums.astype(BF)
            out[z, H:] = split_degree(deg)

    return call(kernel, pltpu.VMEM((NZ, BLK, T), BF), near, other)


def x_sum_kernel(near, other, *refs):
    *parts, out = refs

    @pl.loop(0, NZ)
    def _(z):
        sums, deg = add_blocks([p[z] for p in (near, other, *parts)])
        out[z, :H] = sums.astype(BF)
        out[z, H:] = split_degree(deg)


def x_sum(near, other, parts):
    return call(x_sum_kernel, pltpu.VMEM((NZ, BLK, T), BF), near, other, *parts)


def node_kernel(parts, feats, d_out, w_self, w_neigh, out_feats, d_sum, base, grads, pairs):
    sums, deg = add_blocks([parts[z] for z in range(NZ)])
    deg = 1.0 + deg[:1]
    mean_t = (sums / deg).astype(BF)
    pre = dot(feats[...], w_self[...]) + dot(mean_t, w_neigh[...], TN)
    gate = jax.nn.sigmoid(pre)
    out_feats[...] = (pre * gate).astype(BF)
    d_pre = (d_out[...].astype(F32) * gate * (1.0 + pre * (1.0 - gate))).astype(BF)
    d_sum_t = (dot(w_neigh[...], d_pre, NT) / deg).astype(BF)
    for z in range(NZ):
        d_sum[z] = d_sum_t
    base[...] = dot(w_self[...], d_pre, NT)
    rows = GRAD // 2
    for part, grad in enumerate((dot(feats[...], d_pre, TN), dot(mean_t, d_pre))):
        for g in range(H // rows):
            pairs[g, part * rows : (part + 1) * rows] = grad[g * rows : (g + 1) * rows]
    grads[...] = pairs[...].astype(BF)


def node(parts, feats, d_out, w_self, w_neigh):
    out_shape = (
        jax.ShapeDtypeStruct((T, H), BF),
        pltpu.VMEM((NZ, H, T), BF),
        pltpu.VMEM((H, T), F32),
        pltpu.VMEM((NX * NZ * NC, GRAD, H), BF),
    )
    scratch = [pltpu.VMEM((NX * NZ * NC, GRAD, H), F32)]
    return call(node_kernel, out_shape, parts, feats, d_out, w_self, w_neigh, scratch=scratch)


def backward_sums(far, ids, slots, srcs, pairs, my_x, vals, pieces, start, acc, lhs, buffers):
    def prepare():
        acc[...] = start()
        for k in range(NX):
            lhs[k * NZ : (k + 1) * NZ] = pieces[k][...]

    def block(n):
        back = my_x[0] - (slots[n] >> 3)
        return lhs[(back & (NX - 1)) * NZ + (slots[n] & (NZ - 1))]

    def step(tiles):
        sides = [jnp.concatenate([block(n), block(n + 1)], axis=1) for n, _ in tiles]
        prods = [dot(side, pair) for side, (_, pair) in zip(sides, tiles)]
        for (n, _), prod in zip(tiles, prods):
            acc[srcs[n]] = acc[srcs[n]] + prod

    over_pairs(far, ids, pairs, vals, buffers, prepare, step)


def backward_near_kernel(ids, slots, srcs, pairs, my_x, vals, *refs):
    *pieces, out, lhs, tiles, sems = refs
    zeros = lambda: jnp.zeros(out.shape, F32)
    backward_sums(0, ids, slots, srcs, pairs, my_x, vals, pieces, zeros, out, lhs, (tiles, sems))


def backward_far_kernel(ids, slots, srcs, pairs, my_x, vals, *refs):
    *pieces, near, grads, out, acc, lhs, tiles, sems = refs
    start = lambda: near[...]
    backward_sums(1, ids, slots, srcs, pairs, my_x, vals, pieces, start, acc, lhs, (tiles, sems))
    grad = jnp.sum(grads[...].astype(F32), axis=0)
    high = grad.astype(BF).astype(F32)
    parts = [p[:, k : k + T] for p in (high, grad - high) for k in range(0, H, T)]
    grad_rows = jnp.concatenate(parts, axis=0).astype(BF)
    for s in range(NR):
        out[s, :H] = acc[s].astype(BF)
        out[s, H:] = grad_rows


def backward_near(lists, my_x, tiles, pieces):
    scratch = [pltpu.VMEM((HALF, H, T), BF), *BUFFERS]
    out_shape = pltpu.VMEM((NR, H, T), F32)
    args = (*lists, my_x, tiles, *pieces)
    return call(backward_near_kernel, out_shape, *args, scratch=scratch, cost=BACKWARD_COST)


def backward_far(lists, my_x, tiles, pieces, near, grads):
    scratch = [pltpu.VMEM((NR, H, T), F32), pltpu.VMEM((HALF, H, T), BF), *BUFFERS]
    out_shape = pltpu.VMEM((NR, H + 4 * GRAD, T), BF)
    args = (*lists, my_x, tiles, *pieces, near, grads)
    return call(backward_far_kernel, out_shape, *args, scratch=scratch, cost=BACKWARD_COST)


def final_kernel(parts, base, out, *grads):
    total = parts[0].astype(F32)
    for r in range(1, NR):
        total = total + parts[r].astype(F32)
    out[...] = (base[...] + total[:H]).T.astype(BF)
    rows = GRAD // 2
    for k in range(H // T):
        high, low = (total[H + (2 * p + k) * GRAD :][:GRAD] for p in range(2))
        for part, grad in enumerate(grads):
            grad[:, k * T : (k + 1) * T] = (high + low)[part * rows : (part + 1) * rows]


def final(parts, base):
    grad = jax.ShapeDtypeStruct((GRAD // 2, H), F32)
    return call(final_kernel, (jax.ShapeDtypeStruct((T, H), BF), grad, grad), parts, base)


def shift(size, by):
    return [(i, (i + by) % size) for i in range(size)]


def layer(feats, w_self, w_neigh, tile_vals, tile_owner, tile_src, tile_count, d_out):
    tiles = tile_vals[0, 0]
    my_x = lax.axis_index("x").reshape(1)
    meta = jnp.stack([tile_count[0, 0], lax.axis_index("x"), lax.axis_index("core")])
    swap = shift(NC, 1)

    panel = lax.all_to_all(spread(feats), "rep", 0, 0)
    lists = order(tile_owner[0, 0], tile_src[0, 0], meta)
    far = forward_far(lists, my_x, tiles, panel)
    near = forward_near(lists, my_x, tiles, panel)
    other = lax.ppermute(far, "core", swap)
    parts = [lax.ppermute(core_sum(near, other, k), "x", shift(NX, k)) for k in range(1, NX)]
    mine = lax.all_to_all(x_sum(near, other, parts), "z", 0, 0)

    out_feats, d_sum, base, grads = node(mine, feats, d_out, w_self, w_neigh)

    def shifted(k):
        return lax.ppermute(column, "x", shift(NX, k))

    def swapped(k):
        return lax.ppermute(pieces[k], "core", swap)

    grads = lax.all_to_all(grads, ("x", "z", "core"), 0, 0)
    column = lax.all_to_all(d_sum, "z", 0, 0)
    pieces = [column] + [shifted(k) for k in range(1, NX)]
    others = [swapped(k) for k in range(NX)]
    back = backward_near(lists, my_x, tiles, pieces)
    back = backward_far(lists, my_x, tiles, others, back, grads)
    return (out_feats, *final(lax.all_to_all(back, "rep", 0, 0), base))


def solution(mesh):
    split = Mesh(mesh.devices.reshape(NR, NX, NZ, NC), ("rep", "x", "z", "core"))
    dom = ("x", "z", "core")
    nodes = P(("rep", *dom), None)
    in_specs = (
        nodes,
        P(),
        P(),
        P("rep", dom, None, None, None),
        P("rep", dom, None),
        P("rep", dom, None),
        P("rep", dom),
        nodes,
    )
    out_specs = (nodes, nodes, P(dom, None), P(dom, None))
    return jax.shard_map(layer, mesh=split, in_specs=in_specs, out_specs=out_specs, check_vma=False)
```

```python
import jax
import jax.numpy as jnp
from jax import lax
from jax.experimental import pallas as pl
from jax.experimental.pallas import tpu as pltpu
from jax.sharding import Mesh
from jax.sharding import PartitionSpec as P


BF = jnp.bfloat16
F32 = jnp.float32
NX, NZ, NC, NR = 4, 8, 2, 8
T = 128
H = 256
TILES = 128
SLOTS = 144
UNROLL = 8
HALF = NX * NZ
DEG = 8
GRAD = 8
BLK = H + 2 * DEG
VMEM = pl.BlockSpec(memory_space=pltpu.VMEM)
SMEM = pl.BlockSpec(memory_space=pltpu.SMEM)
HBM = pl.BlockSpec(memory_space=pltpu.HBM)
PARAMS = pltpu.CompilerParams(vmem_limit_bytes=20 * 1024 * 1024)
NT = (((1,), (1,)), ((), ()))
TN = (((0,), (0,)), ((), ()))


def dot(a, b, dims=(((1,), (0,)), ((), ()))):
    return lax.dot_general(a, b, dims, preferred_element_type=F32)


def call(kernel, out_shape, *args, scratch=(), cost=None):
    def spec(a):
        return SMEM if a.dtype == jnp.int32 else HBM if a.shape == (TILES, T, T) else VMEM

    def place(a):
        s = spec(a)
        return a if s is SMEM else pltpu.with_memory_space_constraint(a, s.memory_space)

    args = [place(a) for a in args]
    return pl.pallas_call(
        kernel,
        in_specs=[spec(a) for a in args],
        out_specs=jax.tree.map(spec, out_shape, is_leaf=lambda a: hasattr(a, "dtype")),
        out_shape=out_shape,
        scratch_shapes=scratch,
        compiler_params=PARAMS,
        cost_estimate=cost,
    )(*args)


def split_degree(deg):
    high = deg.astype(BF).astype(F32)
    return jnp.concatenate([high, deg - high], axis=0).astype(BF)


def add_blocks(blocks):
    sums, deg = 0.0, 0.0
    for block in blocks:
        block = block.astype(F32)
        sums = sums + block[:H]
        deg = deg + block[H : H + DEG]
        if block.shape[0] == BLK:
            deg = deg + block[H + DEG :]
    return sums, deg


def spread_kernel(feats, out):
    block = feats[...].astype(F32).T.astype(BF)
    for r in range(NR):
        out[r] = block


def spread(feats):
    return call(spread_kernel, pltpu.VMEM((NR, H, T), BF), feats)


def order_kernel(owners, sources, meta, ids, owner_slots, srcs, steps_of, seen):
    count, my_core = meta[0], meta[2]

    def bucket(t):
        return ((owners[t] & 1) ^ my_core) * NR + sources[t]

    @pl.loop(0, NC * NR)
    def _(b):
        seen[b] = 0

    @pl.loop(0, count)
    def _(t):
        seen[bucket(t)] = seen[bucket(t)] + 1

    for far in range(NC):
        at = jnp.int32(far * SLOTS)
        for src in range(NR):
            size = seen[far * NR + src]
            seen[far * NR + src] = at
            at = at + size

            @pl.when(size % 2 == 1)
            def _():
                ids[at], owner_slots[at], srcs[at] = TILES, 0, src

            at = at + size % 2
        size = at - far * SLOTS
        steps = (size + 2 * UNROLL - 1) // (2 * UNROLL)
        steps_of[far] = steps

        @pl.loop(size, steps * 2 * UNROLL)
        def _(k):
            ids[far * SLOTS + k], owner_slots[far * SLOTS + k], srcs[far * SLOTS + k] = TILES, 0, 0

    @pl.loop(0, count)
    def _(t):
        at = seen[bucket(t)]
        seen[bucket(t)] = at + 1
        ids[at] = t
        owner_slots[at] = owners[t] >> 1
        srcs[at] = sources[t]


def order(owners, sources, meta):
    lists = jax.ShapeDtypeStruct((NC * SLOTS,), jnp.int32)
    out_shape = (lists, lists, lists, jax.ShapeDtypeStruct((NC,), jnp.int32))
    scratch = [pltpu.SMEM((NC * NR,), jnp.int32)]
    return call(order_kernel, out_shape, owners, sources, meta, scratch=scratch)


def with_tiles(vals, tiles, sems, prepare):
    part = TILES // sems.shape[0]
    copies = [
        pltpu.make_async_copy(vals.at[pl.ds(k * part, part)], tiles.at[pl.ds(k * part, part)], sems.at[k])
        for k in range(TILES // part)
    ]
    for copy in copies:
        copy.start()
    tiles[TILES] = jnp.zeros((T, T), BF)
    prepare()
    for copy in copies:
        copy.wait()


def over_pairs(far, ids, steps_of, tiles, step):
    @pl.loop(0, steps_of[far])
    def _(q):
        ns = [far * SLOTS + (q * UNROLL + k) * 2 for k in range(UNROLL)]
        step([(n, jnp.concatenate([tiles[ids[n]], tiles[ids[n + 1]]], axis=0)) for n in ns])


def forward_prepare(panel, acc, lhs):
    acc[...] = jnp.zeros(acc.shape, F32)
    for s in range(NR):
        lhs[s, :H] = panel[s]
        lhs[s, H:] = jnp.ones((2 * DEG, T), BF)


def forward_sums(far, lists, tiles, acc, lhs):
    ids, slots, srcs, steps_of, my_x = lists

    def step(pairs):
        prods = [dot(lhs[srcs[n]], pair, NT) for n, pair in pairs]
        for (n, _), prod in zip(pairs, prods):
            for k in range(2):
                slot = (slots[n + k] - my_x[0] * NZ) & (HALF - 1)
                acc[slot] = acc[slot] + prod[: H + DEG, k * T : (k + 1) * T]

    over_pairs(far, ids, steps_of, tiles, step)


def forward_far_kernel(*refs):
    *lists, vals, panel, out, tiles, acc, lhs, sems = refs
    with_tiles(vals, tiles, sems, lambda: forward_prepare(panel, acc, lhs))
    forward_sums(1, lists, tiles, acc, lhs)

    @pl.loop(0, HALF)
    def _(b):
        out[b, :H] = acc[b, :H].astype(BF)
        out[b, H:] = split_degree(acc[b, H:])


def forward_near_kernel(*refs):
    *lists, tiles, panel, out, lhs = refs
    forward_prepare(panel, out, lhs)
    forward_sums(0, lists, tiles, out, lhs)


COST = pl.CostEstimate(flops=64 * 2 * BLK * T * T, bytes_accessed=2**21, transcendentals=0)
LOADED = pltpu.VMEM((TILES + 1, T, T), BF)
SEMS = pltpu.SemaphoreType.DMA((4,))


def forward_far(lists, vals, panel):
    scratch = [pltpu.VMEM((HALF, H + DEG, T), F32), pltpu.VMEM((NR, BLK, T), BF), SEMS]
    out_shape = (pltpu.VMEM((HALF, BLK, T), BF), LOADED)
    return call(forward_far_kernel, out_shape, *lists, vals, panel, scratch=scratch, cost=COST)


def forward_near(lists, tiles, panel):
    scratch = [pltpu.VMEM((NR, BLK, T), BF)]
    out_shape = pltpu.VMEM((HALF, H + DEG, T), F32)
    return call(forward_near_kernel, out_shape, *lists, tiles, panel, scratch=scratch, cost=COST)


def core_sum(near, other, dx):
    def kernel(a, b, out):
        @pl.loop(0, NZ)
        def _(z):
            sums, deg = add_blocks([a[dx * NZ + z], b[dx * NZ + z]])
            out[z, :H] = sums.astype(BF)
            out[z, H:] = split_degree(deg)

    return call(kernel, pltpu.VMEM((NZ, BLK, T), BF), near, other)


def x_sum_kernel(near, other, *refs):
    *parts, out = refs

    @pl.loop(0, NZ)
    def _(z):
        sums, deg = add_blocks([p[z] for p in (near, other, *parts)])
        out[z, :H] = sums.astype(BF)
        out[z, H:] = split_degree(deg)


def x_sum(near, other, parts):
    return call(x_sum_kernel, pltpu.VMEM((NZ, BLK, T), BF), near, other, *parts)


def node_kernel(parts, feats, d_out, w_self, w_neigh, out_feats, d_sum, base, grads, pairs):
    sums, deg = add_blocks([parts[z] for z in range(NZ)])
    deg = 1.0 + deg[:1]
    mean_t = (sums / deg).astype(BF)
    pre = dot(feats[...], w_self[...]) + dot(mean_t, w_neigh[...], TN)
    gate = jax.nn.sigmoid(pre)
    out_feats[...] = (pre * gate).astype(BF)
    d_pre = (d_out[...].astype(F32) * gate * (1.0 + pre * (1.0 - gate))).astype(BF)
    d_sum_t = (dot(w_neigh[...], d_pre, NT) / deg).astype(BF)
    for z in range(NZ):
        d_sum[z] = d_sum_t
    base[...] = dot(w_self[...], d_pre, NT)
    rows = GRAD // 2
    for part, grad in enumerate((dot(feats[...], d_pre, TN), dot(mean_t, d_pre))):
        for g in range(H // rows):
            pairs[g, part * rows : (part + 1) * rows] = grad[g * rows : (g + 1) * rows]
    grads[...] = pairs[...].astype(BF)


def node(parts, feats, d_out, w_self, w_neigh):
    out_shape = (
        jax.ShapeDtypeStruct((T, H), BF),
        pltpu.VMEM((NZ, H, T), BF),
        pltpu.VMEM((H, T), F32),
        pltpu.VMEM((NX * NZ * NC, GRAD, H), BF),
    )
    scratch = [pltpu.VMEM((NX * NZ * NC, GRAD, H), F32)]
    return call(node_kernel, out_shape, parts, feats, d_out, w_self, w_neigh, scratch=scratch)


def backward_prepare(pieces, start, acc, lhs):
    acc[...] = start
    for k in range(NX):
        lhs[k * NZ : (k + 1) * NZ] = pieces[k][...]


def backward_sums(far, lists, tiles, acc, lhs):
    ids, slots, srcs, steps_of, my_x = lists

    def block(n):
        back = my_x[0] - (slots[n] >> 3)
        return lhs[(back & (NX - 1)) * NZ + (slots[n] & (NZ - 1))]

    def step(pairs):
        sides = [jnp.concatenate([block(n), block(n + 1)], axis=1) for n, _ in pairs]
        prods = [dot(side, pair) for side, (_, pair) in zip(sides, pairs)]
        for (n, _), prod in zip(pairs, prods):
            acc[srcs[n]] = acc[srcs[n]] + prod

    over_pairs(far, ids, steps_of, tiles, step)


def backward_near_kernel(*refs):
    lists, vals, pieces, (out, tiles, lhs, sems) = refs[:5], refs[5], refs[6 : 6 + NX], refs[6 + NX :]
    with_tiles(vals, tiles, sems, lambda: backward_prepare(pieces, jnp.zeros(out.shape, F32), out, lhs))
    backward_sums(0, lists, tiles, out, lhs)


def backward_far_kernel(*refs):
    lists, tiles, pieces, (near, grads, out, acc, lhs) = refs[:5], refs[5], refs[6 : 6 + NX], refs[6 + NX :]
    backward_prepare(pieces, near[...], acc, lhs)
    backward_sums(1, lists, tiles, acc, lhs)
    grad = jnp.sum(grads[...].astype(F32), axis=0)
    high = grad.astype(BF).astype(F32)
    parts = [p[:, k : k + T] for p in (high, grad - high) for k in range(0, H, T)]
    grad_rows = jnp.concatenate(parts, axis=0).astype(BF)
    for s in range(NR):
        out[s, :H] = acc[s].astype(BF)
        out[s, H:] = grad_rows


def backward_near(lists, vals, pieces):
    scratch = [pltpu.VMEM((HALF, H, T), BF), SEMS]
    out_shape = (pltpu.VMEM((NR, H, T), F32), LOADED)
    return call(backward_near_kernel, out_shape, *lists, vals, *pieces, scratch=scratch, cost=COST)


def backward_far(lists, tiles, pieces, near, grads):
    scratch = [pltpu.VMEM((NR, H, T), F32), pltpu.VMEM((HALF, H, T), BF)]
    out_shape = pltpu.VMEM((NR, H + 4 * GRAD, T), BF)
    args = (*lists, tiles, *pieces, near, grads)
    return call(backward_far_kernel, out_shape, *args, scratch=scratch, cost=COST)


def final_kernel(parts, base, out, *grads):
    total = parts[0].astype(F32)
    for r in range(1, NR):
        total = total + parts[r].astype(F32)
    out[...] = (base[...] + total[:H]).T.astype(BF)
    rows = GRAD // 2
    for k in range(H // T):
        high, low = (total[H + (2 * p + k) * GRAD :][:GRAD] for p in range(2))
        for part, grad in enumerate(grads):
            grad[:, k * T : (k + 1) * T] = (high + low)[part * rows : (part + 1) * rows]


def final(parts, base):
    grad = jax.ShapeDtypeStruct((GRAD // 2, H), F32)
    return call(final_kernel, (jax.ShapeDtypeStruct((T, H), BF), grad, grad), parts, base)


def shift(size, by):
    return [(i, (i + by) % size) for i in range(size)]


def layer(feats, w_self, w_neigh, tile_vals, tile_owner, tile_src, tile_count, d_out):
    tiles = tile_vals[0, 0]
    my_x = lax.axis_index("x").reshape(1)
    meta = jnp.stack([tile_count[0, 0], lax.axis_index("x"), lax.axis_index("core")])
    swap = shift(NC, 1)

    panel = lax.all_to_all(spread(feats), "rep", 0, 0)
    lists = (*order(tile_owner[0, 0], tile_src[0, 0], meta), my_x)
    far, loaded = forward_far(lists, tiles, panel)
    near = forward_near(lists, loaded, panel)
    other = lax.ppermute(far, "core", swap)
    parts = [lax.ppermute(core_sum(near, other, k), "x", shift(NX, k)) for k in range(1, NX)]
    mine = lax.all_to_all(x_sum(near, other, parts), "z", 0, 0)

    out_feats, d_sum, base, grads = node(mine, feats, d_out, w_self, w_neigh)

    def shifted(k):
        return lax.ppermute(column, "x", shift(NX, k))

    def swapped(k):
        return lax.ppermute(pieces[k], "core", swap)

    grads = lax.all_to_all(grads, ("x", "z", "core"), 0, 0)
    column = lax.all_to_all(d_sum, "z", 0, 0)
    pieces = [column] + [shifted(k) for k in range(1, NX)]
    others = [swapped(k) for k in range(NX)]
    back, loaded = backward_near(lists, tiles, pieces)
    back = backward_far(lists, loaded, others, back, grads)
    return (out_feats, *final(lax.all_to_all(back, "rep", 0, 0), base))


def solution(mesh):
    split = Mesh(mesh.devices.reshape(NR, NX, NZ, NC), ("rep", "x", "z", "core"))
    dom = ("x", "z", "core")
    nodes = P(("rep", *dom), None)
    in_specs = (
        nodes,
        P(),
        P(),
        P("rep", dom, None, None, None),
        P("rep", dom, None),
        P("rep", dom, None),
        P("rep", dom),
        nodes,
    )
    out_specs = (nodes, nodes, P(dom, None), P(dom, None))
    return jax.shard_map(layer, mesh=split, in_specs=in_specs, out_specs=out_specs, check_vma=False)
```

```python
import jax
import jax.numpy as jnp
from jax import lax
from jax.experimental import pallas as pl
from jax.experimental.pallas import tpu as pltpu
from jax.sharding import Mesh
from jax.sharding import PartitionSpec as P


BF = jnp.bfloat16
F32 = jnp.float32
NX, NZ, NC, NR = 4, 8, 2, 8
T = 128
H = 256
TILES = 128
SLOTS = 144
UNROLL = 8
HALF = NX * NZ
DEG = 8
GRAD = 8
GROWS = 2 * GRAD
BLK = H + 2 * DEG
VMEM = pl.BlockSpec(memory_space=pltpu.VMEM)
SMEM = pl.BlockSpec(memory_space=pltpu.SMEM)
HBM = pl.BlockSpec(memory_space=pltpu.HBM)
PARAMS = pltpu.CompilerParams(vmem_limit_bytes=20 * 1024 * 1024)
NT = (((1,), (1,)), ((), ()))
TN = (((0,), (0,)), ((), ()))


def dot(a, b, dims=(((1,), (0,)), ((), ()))):
    return lax.dot_general(a, b, dims, preferred_element_type=F32)


def call(kernel, name, out_shape, *args, scratch=(), cost=None):
    def spec(a):
        return SMEM if a.dtype == jnp.int32 else HBM if a.shape == (TILES, T, T) else VMEM

    def place(a):
        s = spec(a)
        return a if s is SMEM else pltpu.with_memory_space_constraint(a, s.memory_space)

    args = [place(a) for a in args]
    return pl.pallas_call(
        kernel,
        in_specs=[spec(a) for a in args],
        out_specs=jax.tree.map(spec, out_shape, is_leaf=lambda a: hasattr(a, "dtype")),
        out_shape=out_shape,
        scratch_shapes=scratch,
        compiler_params=PARAMS,
        cost_estimate=cost,
        name=name,
    )(*args)


def add_blocks(blocks):
    sums, deg = 0.0, 0.0
    for block in blocks:
        block = block.astype(F32)
        sums = sums + block[:H]
        deg = deg + block[H : H + DEG]
        if block.shape[0] == BLK:
            deg = deg + block[H + DEG :]
    return sums, deg


def fold(rows):
    return jnp.concatenate([rows[:, k : k + T] for k in range(0, H, T)], axis=0)


def two_parts(rows):
    high = rows.astype(BF).astype(F32)
    return jnp.concatenate([high, rows - high], axis=0).astype(BF)


def spread_kernel(feats, out):
    block = feats[...].astype(F32).T.astype(BF)
    for r in range(NR):
        out[r] = block


def spread(feats):
    return call(spread_kernel, "spread", pltpu.VMEM((NR, H, T), BF), feats)


def order_kernel(owners, sources, counts, cores, ids, owner_slots, srcs, steps_of, seen):
    count, my_core = counts[0], cores[0]

    def bucket(t):
        return ((owners[t] & 1) ^ my_core) * NR + sources[t]

    @pl.loop(0, NC * NR)
    def _(b):
        seen[b] = 0

    @pl.loop(0, count)
    def _(t):
        seen[bucket(t)] = seen[bucket(t)] + 1

    for far in range(NC):
        at = jnp.int32(far * SLOTS)
        for src in range(NR):
            size = seen[far * NR + src]
            seen[far * NR + src] = at
            at = at + size

            @pl.when(size % 2 == 1)
            def _():
                ids[at], owner_slots[at], srcs[at] = TILES, 0, src

            at = at + size % 2
        size = at - far * SLOTS
        steps = (size + 2 * UNROLL - 1) // (2 * UNROLL)
        steps_of[far] = steps

        @pl.loop(size, steps * 2 * UNROLL)
        def _(k):
            ids[far * SLOTS + k], owner_slots[far * SLOTS + k], srcs[far * SLOTS + k] = TILES, 0, 0

    @pl.loop(0, count)
    def _(t):
        at = seen[bucket(t)]
        seen[bucket(t)] = at + 1
        ids[at] = t
        owner_slots[at] = owners[t] >> 1
        srcs[at] = sources[t]


def order(owners, sources, counts, cores):
    lists = jax.ShapeDtypeStruct((NC * SLOTS,), jnp.int32)
    out_shape = (lists, lists, lists, jax.ShapeDtypeStruct((NC,), jnp.int32))
    scratch = [pltpu.SMEM((NC * NR,), jnp.int32)]
    return call(order_kernel, "order", out_shape, owners, sources, counts, cores, scratch=scratch)


def with_tiles(vals, tiles, sems, prepare):
    part = TILES // sems.shape[0]
    copies = [
        pltpu.make_async_copy(vals.at[pl.ds(k * part, part)], tiles.at[pl.ds(k * part, part)], sems.at[k])
        for k in range(TILES // part)
    ]
    for copy in copies:
        copy.start()
    tiles[TILES] = jnp.zeros((T, T), BF)
    prepare()
    for copy in copies:
        copy.wait()


def over_pairs(far, ids, steps_of, tiles, step):
    @pl.loop(0, steps_of[far])
    def _(q):
        ns = [far * SLOTS + (q * UNROLL + k) * 2 for k in range(UNROLL)]
        step([(n, jnp.concatenate([tiles[ids[n]], tiles[ids[n + 1]]], axis=0)) for n in ns])


def forward_prepare(panel, acc, lhs):
    acc[...] = jnp.zeros(acc.shape, F32)
    for s in range(NR):
        lhs[s, :H] = panel[s]
        lhs[s, H:] = jnp.ones((2 * DEG, T), BF)


def forward_sums(far, lists, tiles, acc, lhs):
    ids, slots, srcs, steps_of, _ = lists

    def step(pairs):
        prods = [dot(lhs[srcs[n]], pair, NT) for n, pair in pairs]
        for (n, _), prod in zip(pairs, prods):
            for k in range(2):
                slot = slots[n + k]
                acc[slot] = acc[slot] + prod[: H + DEG, k * T : (k + 1) * T]

    over_pairs(far, ids, steps_of, tiles, step)


def forward_far_kernel(*refs):
    *lists, vals, panel, out, tiles, acc, lhs, sems = refs
    with_tiles(vals, tiles, sems, lambda: forward_prepare(panel, acc, lhs))
    forward_sums(1, lists, tiles, acc, lhs)

    @pl.loop(0, HALF)
    def _(b):
        out[b, :H] = acc[b, :H].astype(BF)
        out[b, H:] = two_parts(acc[b, H:])


def forward_near_kernel(*refs):
    *lists, tiles, panel, out, lhs = refs
    forward_prepare(panel, out, lhs)
    forward_sums(0, lists, tiles, out, lhs)


COST = pl.CostEstimate(flops=64 * 2 * BLK * T * T, bytes_accessed=2**21, transcendentals=0)
LOADED = pltpu.VMEM((TILES + 1, T, T), BF)
SEMS = pltpu.SemaphoreType.DMA((4,))


def forward_far(lists, vals, panel):
    scratch = [pltpu.VMEM((HALF, H + DEG, T), F32), pltpu.VMEM((NR, BLK, T), BF), SEMS]
    out_shape = (pltpu.VMEM((HALF, BLK, T), BF), LOADED)
    return call(forward_far_kernel, "forward_far", out_shape, *lists, vals, panel, scratch=scratch, cost=COST)


def forward_near(lists, tiles, panel):
    scratch = [pltpu.VMEM((NR, BLK, T), BF)]
    out_shape = pltpu.VMEM((HALF, H + DEG, T), F32)
    return call(forward_near_kernel, "forward_near", out_shape, *lists, tiles, panel, scratch=scratch, cost=COST)


def core_sum_kernel(near, other, out):
    @pl.loop(0, NZ)
    def _(z):
        for x in range(NX):
            sums, deg = add_blocks([near[x * NZ + z], other[x * NZ + z]])
            out[x, z, :H] = sums.astype(BF)
            out[x, z, H:] = two_parts(deg)


def core_sum(near, other):
    return call(core_sum_kernel, "core_sum", pltpu.VMEM((NX, NZ, BLK, T), BF), near, other)


def x_sum_kernel(parts, out):
    @pl.loop(0, NZ)
    def _(z):
        sums, deg = add_blocks([parts[x, z] for x in range(NX)])
        out[z, :H] = sums.astype(BF)
        out[z, H:] = two_parts(deg)


def x_sum(parts):
    return call(x_sum_kernel, "x_sum", pltpu.VMEM((NZ, BLK, T), BF), parts)


def node_kernel(parts, feats, d_out, w_self, w_neigh, out_feats, d_sum, base, pairs):
    sums, deg = add_blocks([parts[z] for z in range(NZ)])
    deg = 1.0 + deg[:1]
    mean_t = (sums / deg).astype(BF)
    pre = dot(feats[...], w_self[...]) + dot(mean_t, w_neigh[...], TN)
    gate = jax.nn.sigmoid(pre)
    out_feats[...] = (pre * gate).astype(BF)
    d_pre = (d_out[...].astype(F32) * gate * (1.0 + pre * (1.0 - gate))).astype(BF)
    d_sum_t = (dot(w_neigh[...], d_pre, NT) / deg).astype(BF)
    for z in range(NZ):
        d_sum[z, :H] = d_sum_t
    base[...] = dot(w_self[...], d_pre, NT)
    rows = GRAD // 2
    for part, grad in enumerate((dot(feats[...], d_pre, TN), dot(mean_t, d_pre))):
        for g in range(H // rows):
            pairs[g, part * rows : (part + 1) * rows] = grad[g * rows : (g + 1) * rows]
    for z in range(NZ):
        for j in range(NX * NC):
            d = (j // NC * NZ + z) * NC + j % NC
            d_sum[z, H + j * GROWS : H + (j + 1) * GROWS] = fold(pairs[d]).astype(BF)


def node(parts, feats, d_out, w_self, w_neigh):
    out_shape = (
        jax.ShapeDtypeStruct((T, H), BF),
        pltpu.VMEM((NZ, H + NX * NC * GROWS, T), BF),
        pltpu.VMEM((H, T), F32),
    )
    scratch = [pltpu.VMEM((NX * NZ * NC, GRAD, H), F32)]
    return call(node_kernel, "node", out_shape, parts, feats, d_out, w_self, w_neigh, scratch=scratch)


def copies_kernel(parts, out):
    grads = jnp.zeros((NX * NC * GROWS, T), F32)
    for z in range(NZ):
        grads = grads + parts[z, H:].astype(F32)
        for x in range(NX):
            out[x, z * H : (z + 1) * H] = parts[z, :H]
    for j in range(NX * NC):
        at = NZ * H + j % NC * 2 * GROWS
        out[j // NC, at : at + 2 * GROWS] = two_parts(grads[j * GROWS : (j + 1) * GROWS])


def copies(parts):
    out_shape = pltpu.VMEM((NX, NZ * H + NC * 2 * GROWS, T), BF)
    return call(copies_kernel, "copies", out_shape, parts)


def own_gradients(blocks, my_core):
    at = pl.multiple_of(NZ * H + my_core * 2 * GROWS, 2 * GROWS)
    total = 0.0
    for x in range(NX):
        both = blocks[x, pl.ds(at, 2 * GROWS)].astype(F32)
        total = total + both[:GROWS] + both[GROWS:]
    return total


def backward_sums(far, lists, tiles, blocks, acc):
    ids, slots, srcs, steps_of, _ = lists

    def block(n):
        return blocks[slots[n] >> 3, pl.ds(pl.multiple_of((slots[n] & (NZ - 1)) * H, H), H)]

    def step(pairs):
        sides = [jnp.concatenate([block(n), block(n + 1)], axis=1) for n, _ in pairs]
        prods = [dot(side, pair) for side, (_, pair) in zip(sides, pairs)]
        for (n, _), prod in zip(pairs, prods):
            acc[srcs[n]] = acc[srcs[n]] + prod

    over_pairs(far, ids, steps_of, tiles, step)


def backward_near_kernel(*refs):
    *lists, tiles, blocks, out, grads = refs
    out[...] = jnp.zeros(out.shape, F32)
    grads[...] = own_gradients(blocks, lists[4][0])
    backward_sums(0, lists, tiles, blocks, out)


def backward_far_kernel(*refs):
    *lists, tiles, blocks, near, grads, out, acc = refs
    acc[...] = near[...]
    backward_sums(1, lists, tiles, blocks, acc)
    grad_rows = two_parts(grads[...] + own_gradients(blocks, lists[4][0]))
    for s in range(NR):
        out[s, :H] = acc[s].astype(BF)
        out[s, H:] = grad_rows


def backward_near(lists, tiles, blocks):
    out_shape = (pltpu.VMEM((NR, H, T), F32), pltpu.VMEM((GROWS, T), F32))
    return call(backward_near_kernel, "backward_near", out_shape, *lists, tiles, blocks, cost=COST)


def backward_far(lists, tiles, blocks, near, grads):
    scratch = [pltpu.VMEM((NR, H, T), F32)]
    out_shape = pltpu.VMEM((NR, H + 2 * GROWS, T), BF)
    args = (*lists, tiles, blocks, near, grads)
    return call(backward_far_kernel, "backward_far", out_shape, *args, scratch=scratch, cost=COST)


def final_kernel(parts, base, out, *grads):
    total = parts[0].astype(F32)
    for r in range(1, NR):
        total = total + parts[r].astype(F32)
    out[...] = (base[...] + total[:H]).T.astype(BF)
    rows = GRAD // 2
    for k in range(H // T):
        high, low = (total[H + (2 * p + k) * GRAD :][:GRAD] for p in range(2))
        for part, grad in enumerate(grads):
            grad[:, k * T : (k + 1) * T] = (high + low)[part * rows : (part + 1) * rows]


def final(parts, base):
    grad = jax.ShapeDtypeStruct((GRAD // 2, H), F32)
    return call(final_kernel, "final", (jax.ShapeDtypeStruct((T, H), BF), grad, grad), parts, base)


def shift(size, by):
    return [(i, (i + by) % size) for i in range(size)]


def per_device(feats, w_self, w_neigh, tile_vals, tile_owner, tile_src, tile_count, d_out):
    tiles, owners, sources = tile_vals[0, 0], tile_owner[0, 0], tile_src[0, 0]
    my_core = lax.axis_index("core").reshape(1)
    swap = shift(NC, 1)

    panel = lax.all_to_all(spread(feats), "rep", 0, 0)
    lists = (*order(owners, sources, tile_count[0], my_core), my_core)
    far, loaded = forward_far(lists, tiles, panel)
    near = forward_near(lists, loaded, panel)
    parts = core_sum(near, lax.ppermute(far, "core", swap))
    parts = x_sum(lax.all_to_all(parts, "x", 0, 0))
    parts = lax.all_to_all(parts, "z", 0, 0)

    out_feats, d_sum, base = node(parts, feats, d_out, w_self, w_neigh)

    column = copies(lax.all_to_all(d_sum, "z", 0, 0))
    blocks = lax.all_to_all(column, "x", 0, 0)
    others = lax.ppermute(blocks, "core", swap)
    back, grads = backward_near(lists, loaded, blocks)
    back = backward_far(lists, loaded, others, back, grads)
    return (out_feats, *final(lax.all_to_all(back, "rep", 0, 0), base))


def solution(mesh):
    split = Mesh(mesh.devices.reshape(NR, NX, NZ, NC), ("rep", "x", "z", "core"))
    dom = ("x", "z", "core")
    nodes = P(("rep", *dom), None)
    in_specs = (
        nodes,
        P(),
        P(),
        P("rep", dom, None, None, None),
        P("rep", dom, None),
        P("rep", dom, None),
        P("rep", dom),
        nodes,
    )
    out_specs = (nodes, nodes, P(dom, None), P(dom, None))
    return jax.shard_map(
        per_device, mesh=split, in_specs=in_specs, out_specs=out_specs, check_vma=False
    )
```

```python
import jax
import jax.numpy as jnp
from jax import lax
from jax.experimental import pallas as pl
from jax.experimental.pallas import tpu as pltpu
from jax.sharding import Mesh
from jax.sharding import PartitionSpec as P


BF = jnp.bfloat16
F32 = jnp.float32
NX, NB, NA, NC, NR = 4, 4, 2, 2, 8
NP = NX * NA
T = 128
H = 256
TILES = 128
SLOTS = 144
UNROLL = 8
HALF = NP * NB
DEG = 8
GRAD = 8
GROWS = 2 * GRAD
BLK = H + 2 * DEG
VMEM = pl.BlockSpec(memory_space=pltpu.VMEM)
SMEM = pl.BlockSpec(memory_space=pltpu.SMEM)
HBM = pl.BlockSpec(memory_space=pltpu.HBM)
PARAMS = pltpu.CompilerParams(vmem_limit_bytes=20 * 1024 * 1024)
NT = (((1,), (1,)), ((), ()))
TN = (((0,), (0,)), ((), ()))


def dot(a, b, dims=(((1,), (0,)), ((), ()))):
    return lax.dot_general(a, b, dims, preferred_element_type=F32)


def call(kernel, name, out_shape, *args, scratch=(), cost=None):
    def spec(a):
        return SMEM if a.dtype == jnp.int32 else HBM if a.shape == (TILES, T, T) else VMEM

    def place(a):
        s = spec(a)
        return a if s is SMEM else pltpu.with_memory_space_constraint(a, s.memory_space)

    args = [place(a) for a in args]
    return pl.pallas_call(
        kernel,
        in_specs=[spec(a) for a in args],
        out_specs=jax.tree.map(spec, out_shape, is_leaf=lambda a: hasattr(a, "dtype")),
        out_shape=out_shape,
        scratch_shapes=scratch,
        compiler_params=PARAMS,
        cost_estimate=cost,
        name=name,
    )(*args)


def add_blocks(blocks):
    sums, deg = 0.0, 0.0
    for block in blocks:
        block = block.astype(F32)
        sums = sums + block[:H]
        deg = deg + block[H : H + DEG]
        if block.shape[0] == BLK:
            deg = deg + block[H + DEG :]
    return sums, deg


def fold(rows):
    return jnp.concatenate([rows[:, k : k + T] for k in range(0, H, T)], axis=0)


def two_parts(rows):
    high = rows.astype(BF).astype(F32)
    return jnp.concatenate([high, rows - high], axis=0).astype(BF)


def spread_kernel(feats, out):
    block = feats[...].astype(F32).T.astype(BF)
    for r in range(NR):
        out[r] = block


def spread(feats):
    return call(spread_kernel, "spread", pltpu.VMEM((NR, H, T), BF), feats)


def order_kernel(owners, sources, counts, cores, ids, owner_slots, srcs, steps_of, seen):
    count, my_core = counts[0], cores[0]

    def bucket(t):
        return ((owners[t] & 1) ^ my_core) * NR + sources[t]

    @pl.loop(0, NC * NR)
    def _(b):
        seen[b] = 0

    @pl.loop(0, count)
    def _(t):
        seen[bucket(t)] = seen[bucket(t)] + 1

    for far in range(NC):
        at = jnp.int32(far * SLOTS)
        for src in range(NR):
            size = seen[far * NR + src]
            seen[far * NR + src] = at
            at = at + size

            @pl.when(size % 2 == 1)
            def _():
                ids[at], owner_slots[at], srcs[at] = TILES, 0, src

            at = at + size % 2
        size = at - far * SLOTS
        steps = (size + 2 * UNROLL - 1) // (2 * UNROLL)
        steps_of[far] = steps

        @pl.loop(size, steps * 2 * UNROLL)
        def _(k):
            ids[far * SLOTS + k], owner_slots[far * SLOTS + k], srcs[far * SLOTS + k] = TILES, 0, 0

    @pl.loop(0, count)
    def _(t):
        at = seen[bucket(t)]
        seen[bucket(t)] = at + 1
        ids[at] = t
        x, zb, za = owners[t] >> 4, (owners[t] >> 2) & 3, (owners[t] >> 1) & 1
        owner_slots[at] = (x * NA + za) * NB + zb
        srcs[at] = sources[t]


def order(owners, sources, counts, cores):
    lists = jax.ShapeDtypeStruct((NC * SLOTS,), jnp.int32)
    out_shape = (lists, lists, lists, jax.ShapeDtypeStruct((NC,), jnp.int32))
    scratch = [pltpu.SMEM((NC * NR,), jnp.int32)]
    return call(order_kernel, "order", out_shape, owners, sources, counts, cores, scratch=scratch)


def with_tiles(vals, tiles, sems, prepare):
    part = TILES // sems.shape[0]
    copies = [
        pltpu.make_async_copy(vals.at[pl.ds(k * part, part)], tiles.at[pl.ds(k * part, part)], sems.at[k])
        for k in range(TILES // part)
    ]
    for copy in copies:
        copy.start()
    tiles[TILES] = jnp.zeros((T, T), BF)
    prepare()
    for copy in copies:
        copy.wait()


def over_pairs(far, ids, steps_of, tiles, step):
    @pl.loop(0, steps_of[far])
    def _(q):
        ns = [far * SLOTS + (q * UNROLL + k) * 2 for k in range(UNROLL)]
        step([(n, jnp.concatenate([tiles[ids[n]], tiles[ids[n + 1]]], axis=0)) for n in ns])


def forward_prepare(panel, acc, lhs):
    acc[...] = jnp.zeros(acc.shape, F32)
    for s in range(NR):
        lhs[s, :H] = panel[s]
        lhs[s, H:] = jnp.ones((2 * DEG, T), BF)


def forward_sums(far, lists, tiles, acc, lhs):
    ids, slots, srcs, steps_of, _ = lists

    def step(pairs):
        prods = [dot(lhs[srcs[n]], pair, NT) for n, pair in pairs]
        for (n, _), prod in zip(pairs, prods):
            for k in range(2):
                slot = slots[n + k]
                acc[slot] = acc[slot] + prod[: H + DEG, k * T : (k + 1) * T]

    over_pairs(far, ids, steps_of, tiles, step)


def forward_far_kernel(*refs):
    *lists, vals, panel, out, tiles, acc, lhs, sems = refs
    with_tiles(vals, tiles, sems, lambda: forward_prepare(panel, acc, lhs))
    forward_sums(1, lists, tiles, acc, lhs)

    @pl.loop(0, HALF)
    def _(b):
        out[b, :H] = acc[b, :H].astype(BF)
        out[b, H:] = two_parts(acc[b, H:])


def forward_near_kernel(*refs):
    *lists, tiles, panel, out, lhs = refs
    forward_prepare(panel, out, lhs)
    forward_sums(0, lists, tiles, out, lhs)


COST = pl.CostEstimate(flops=64 * 2 * BLK * T * T, bytes_accessed=2**21, transcendentals=0)
LOADED = pltpu.VMEM((TILES + 1, T, T), BF)
SEMS = pltpu.SemaphoreType.DMA((4,))


def forward_far(lists, vals, panel):
    scratch = [pltpu.VMEM((HALF, H + DEG, T), F32), pltpu.VMEM((NR, BLK, T), BF), SEMS]
    out_shape = (pltpu.VMEM((HALF, BLK, T), BF), LOADED)
    return call(forward_far_kernel, "forward_far", out_shape, *lists, vals, panel, scratch=scratch, cost=COST)


def forward_near(lists, tiles, panel):
    scratch = [pltpu.VMEM((NR, BLK, T), BF)]
    out_shape = pltpu.VMEM((HALF, H + DEG, T), F32)
    return call(forward_near_kernel, "forward_near", out_shape, *lists, tiles, panel, scratch=scratch, cost=COST)


def core_sum_kernel(near, other, out):
    @pl.loop(0, NB)
    def _(z):
        for x in range(NP):
            sums, deg = add_blocks([near[x * NB + z], other[x * NB + z]])
            out[x, z, :H] = sums.astype(BF)
            out[x, z, H:] = two_parts(deg)


def core_sum(near, other):
    return call(core_sum_kernel, "core_sum", pltpu.VMEM((NP, NB, BLK, T), BF), near, other)


def x_sum_kernel(parts, out):
    @pl.loop(0, NB)
    def _(z):
        sums, deg = add_blocks([parts[x, z] for x in range(NP)])
        out[z, :H] = sums.astype(BF)
        out[z, H:] = two_parts(deg)


def x_sum(parts):
    return call(x_sum_kernel, "x_sum", pltpu.VMEM((NB, BLK, T), BF), parts)


def node_kernel(parts, feats, d_out, w_self, w_neigh, out_feats, d_sum, base, pairs):
    sums, deg = add_blocks([parts[z] for z in range(NB)])
    deg = 1.0 + deg[:1]
    mean_t = (sums / deg).astype(BF)
    pre = dot(feats[...], w_self[...]) + dot(mean_t, w_neigh[...], TN)
    gate = jax.nn.sigmoid(pre)
    out_feats[...] = (pre * gate).astype(BF)
    d_pre = (d_out[...].astype(F32) * gate * (1.0 + pre * (1.0 - gate))).astype(BF)
    d_sum_t = (dot(w_neigh[...], d_pre, NT) / deg).astype(BF)
    for z in range(NB):
        d_sum[z, :H] = d_sum_t
    base[...] = dot(w_self[...], d_pre, NT)
    rows = GRAD // 2
    for part, grad in enumerate((dot(feats[...], d_pre, TN), dot(mean_t, d_pre))):
        for g in range(H // rows):
            pairs[g, part * rows : (part + 1) * rows] = grad[g * rows : (g + 1) * rows]
    for z in range(NB):
        for j in range(NP * NC):
            x, za, c = j // (NA * NC), j // NC % NA, j % NC
            d = ((x * NB + z) * NA + za) * NC + c
            d_sum[z, H + j * GROWS : H + (j + 1) * GROWS] = fold(pairs[d]).astype(BF)


def node(parts, feats, d_out, w_self, w_neigh):
    out_shape = (
        jax.ShapeDtypeStruct((T, H), BF),
        pltpu.VMEM((NB, H + NP * NC * GROWS, T), BF),
        pltpu.VMEM((H, T), F32),
    )
    scratch = [pltpu.VMEM((NP * NB * NC, GRAD, H), F32)]
    return call(node_kernel, "node", out_shape, parts, feats, d_out, w_self, w_neigh, scratch=scratch)


def copies_kernel(parts, out):
    grads = jnp.zeros((NP * NC * GROWS, T), F32)
    for z in range(NB):
        grads = grads + parts[z, H:].astype(F32)
        for x in range(NP):
            out[x, z * H : (z + 1) * H] = parts[z, :H]
    for j in range(NP * NC):
        at = NB * H + j % NC * 2 * GROWS
        out[j // NC, at : at + 2 * GROWS] = two_parts(grads[j * GROWS : (j + 1) * GROWS])


def copies(parts):
    out_shape = pltpu.VMEM((NP, NB * H + NC * 2 * GROWS, T), BF)
    return call(copies_kernel, "copies", out_shape, parts)


def own_gradients(blocks, my_core):
    at = pl.multiple_of(NB * H + my_core * 2 * GROWS, 2 * GROWS)
    total = 0.0
    for x in range(NP):
        both = blocks[x, pl.ds(at, 2 * GROWS)].astype(F32)
        total = total + both[:GROWS] + both[GROWS:]
    return total


def backward_sums(far, lists, tiles, blocks, acc):
    ids, slots, srcs, steps_of, _ = lists

    def block(n):
        return blocks[slots[n] // NB, pl.ds(pl.multiple_of((slots[n] & (NB - 1)) * H, H), H)]

    def step(pairs):
        sides = [jnp.concatenate([block(n), block(n + 1)], axis=1) for n, _ in pairs]
        prods = [dot(side, pair) for side, (_, pair) in zip(sides, pairs)]
        for (n, _), prod in zip(pairs, prods):
            acc[srcs[n]] = acc[srcs[n]] + prod

    over_pairs(far, ids, steps_of, tiles, step)


def backward_near_kernel(*refs):
    *lists, tiles, blocks, out, grads = refs
    out[...] = jnp.zeros(out.shape, F32)
    grads[...] = own_gradients(blocks, lists[4][0])
    backward_sums(0, lists, tiles, blocks, out)


def backward_far_kernel(*refs):
    *lists, tiles, blocks, near, grads, out, acc = refs
    acc[...] = near[...]
    backward_sums(1, lists, tiles, blocks, acc)
    grad_rows = two_parts(grads[...] + own_gradients(blocks, lists[4][0]))
    for s in range(NR):
        out[s, :H] = acc[s].astype(BF)
        out[s, H:] = grad_rows


def backward_near(lists, tiles, blocks):
    out_shape = (pltpu.VMEM((NR, H, T), F32), pltpu.VMEM((GROWS, T), F32))
    return call(backward_near_kernel, "backward_near", out_shape, *lists, tiles, blocks, cost=COST)


def backward_far(lists, tiles, blocks, near, grads):
    scratch = [pltpu.VMEM((NR, H, T), F32)]
    out_shape = pltpu.VMEM((NR, H + 2 * GROWS, T), BF)
    args = (*lists, tiles, blocks, near, grads)
    return call(backward_far_kernel, "backward_far", out_shape, *args, scratch=scratch, cost=COST)


def final_kernel(parts, base, out, *grads):
    total = parts[0].astype(F32)
    for r in range(1, NR):
        total = total + parts[r].astype(F32)
    out[...] = (base[...] + total[:H]).T.astype(BF)
    rows = GRAD // 2
    for k in range(H // T):
        high, low = (total[H + (2 * p + k) * GRAD :][:GRAD] for p in range(2))
        for part, grad in enumerate(grads):
            grad[:, k * T : (k + 1) * T] = (high + low)[part * rows : (part + 1) * rows]


def final(parts, base):
    grad = jax.ShapeDtypeStruct((GRAD // 2, H), F32)
    return call(final_kernel, "final", (jax.ShapeDtypeStruct((T, H), BF), grad, grad), parts, base)


def shift(size, by):
    return [(i, (i + by) % size) for i in range(size)]


def per_device(feats, w_self, w_neigh, tile_vals, tile_owner, tile_src, tile_count, d_out):
    tiles, owners, sources = tile_vals[0, 0], tile_owner[0, 0], tile_src[0, 0]
    my_core = lax.axis_index("core").reshape(1)
    swap = shift(NC, 1)

    panel = lax.all_to_all(spread(feats), "rep", 0, 0)
    lists = (*order(owners, sources, tile_count[0], my_core), my_core)
    far, loaded = forward_far(lists, tiles, panel)
    near = forward_near(lists, loaded, panel)
    parts = core_sum(near, lax.ppermute(far, "core", swap))
    parts = x_sum(lax.all_to_all(parts, ("x", "za"), 0, 0))
    parts = lax.all_to_all(parts, "zb", 0, 0)

    out_feats, d_sum, base = node(parts, feats, d_out, w_self, w_neigh)

    column = copies(lax.all_to_all(d_sum, "zb", 0, 0))
    blocks = lax.all_to_all(column, ("x", "za"), 0, 0)
    others = lax.ppermute(blocks, "core", swap)
    back, grads = backward_near(lists, loaded, blocks)
    back = backward_far(lists, loaded, others, back, grads)
    return (out_feats, *final(lax.all_to_all(back, "rep", 0, 0), base))


def solution(mesh):
    split = Mesh(mesh.devices.reshape(NR, NX, NB, NA, NC), ("rep", "x", "zb", "za", "core"))
    dom = ("x", "zb", "za", "core")
    nodes = P(("rep", *dom), None)
    in_specs = (
        nodes,
        P(),
        P(),
        P("rep", dom, None, None, None),
        P("rep", dom, None),
        P("rep", dom, None),
        P("rep", dom),
        nodes,
    )
    out_specs = (nodes, nodes, P(dom, None), P(dom, None))
    return jax.shard_map(
        per_device, mesh=split, in_specs=in_specs, out_specs=out_specs, check_vma=False
    )
```

```python
import jax
import jax.numpy as jnp
from jax import lax
from jax.experimental import pallas as pl
from jax.experimental.pallas import tpu as pltpu
from jax.sharding import PartitionSpec as P


BF = jnp.bfloat16
F32 = jnp.float32
NX, NB, NA, NC, NR = 4, 4, 2, 2, 8
NP = NX * NA
T = 128
H = 256
TILES = 128
SLOTS = 144
UNROLL = 8
HALF = NP * NB
DEG = 8
GRAD = 8
GROWS = 2 * GRAD
BLK = H + 2 * DEG
VMEM = pl.BlockSpec(memory_space=pltpu.VMEM)
SMEM = pl.BlockSpec(memory_space=pltpu.SMEM)
HBM = pl.BlockSpec(memory_space=pltpu.HBM)
PARAMS = pltpu.CompilerParams(vmem_limit_bytes=20 * 1024 * 1024)
NT = (((1,), (1,)), ((), ()))
TN = (((0,), (0,)), ((), ()))


def dot(a, b, dims=(((1,), (0,)), ((), ()))):
    return lax.dot_general(a, b, dims, preferred_element_type=F32)


def call(kernel, name, out_shape, *args, scratch=(), cost=None):
    def spec(a):
        return SMEM if a.dtype == jnp.int32 else HBM if a.shape == (TILES, T, T) else VMEM

    def place(a):
        s = spec(a)
        return a if s is SMEM else pltpu.with_memory_space_constraint(a, s.memory_space)

    args = [place(a) for a in args]
    return pl.pallas_call(
        kernel,
        in_specs=[spec(a) for a in args],
        out_specs=jax.tree.map(spec, out_shape, is_leaf=lambda a: hasattr(a, "dtype")),
        out_shape=out_shape,
        scratch_shapes=scratch,
        compiler_params=PARAMS,
        cost_estimate=cost,
        name=name,
    )(*args)


def add_blocks(blocks):
    sums, deg = 0.0, 0.0
    for block in blocks:
        block = block.astype(F32)
        sums = sums + block[:H]
        deg = deg + block[H : H + DEG]
        if block.shape[0] == BLK:
            deg = deg + block[H + DEG :]
    return sums, deg


def fold(rows):
    return jnp.concatenate([rows[:, k : k + T] for k in range(0, H, T)], axis=0)


def two_parts(rows):
    high = rows.astype(BF).astype(F32)
    return jnp.concatenate([high, rows - high], axis=0).astype(BF)


def spread_kernel(feats, out):
    block = feats[...].astype(F32).T.astype(BF)
    for r in range(NR):
        out[r] = block


def spread(feats):
    return call(spread_kernel, "spread", pltpu.VMEM((NR, H, T), BF), feats)


def order_kernel(owners, sources, counts, cores, ids, owner_slots, srcs, steps_of, seen):
    count, my_core = counts[0], cores[0]

    def bucket(t):
        return ((owners[t] & 1) ^ my_core) * NR + sources[t]

    @pl.loop(0, NC * NR)
    def _(b):
        seen[b] = 0

    @pl.loop(0, count)
    def _(t):
        seen[bucket(t)] = seen[bucket(t)] + 1

    for far in range(NC):
        at = jnp.int32(far * SLOTS)
        for src in range(NR):
            size = seen[far * NR + src]
            seen[far * NR + src] = at
            at = at + size

            @pl.when(size % 2 == 1)
            def _():
                ids[at], owner_slots[at], srcs[at] = TILES, 0, src

            at = at + size % 2
        size = at - far * SLOTS
        steps = (size + 2 * UNROLL - 1) // (2 * UNROLL)
        steps_of[far] = steps

        @pl.loop(size, steps * 2 * UNROLL)
        def _(k):
            ids[far * SLOTS + k], owner_slots[far * SLOTS + k], srcs[far * SLOTS + k] = TILES, 0, 0

    @pl.loop(0, count)
    def _(t):
        at = seen[bucket(t)]
        seen[bucket(t)] = at + 1
        ids[at] = t
        x, z = owners[t] >> 4, ((owners[t] >> 1) - (owners[t] & 1)) & (NA * NB - 1)
        owner_slots[at] = (x * NA + (z & 1)) * NB + (z >> 1)
        srcs[at] = sources[t]


def order(owners, sources, counts, cores):
    lists = jax.ShapeDtypeStruct((NC * SLOTS,), jnp.int32)
    out_shape = (lists, lists, lists, jax.ShapeDtypeStruct((NC,), jnp.int32))
    scratch = [pltpu.SMEM((NC * NR,), jnp.int32)]
    return call(order_kernel, "order", out_shape, owners, sources, counts, cores, scratch=scratch)


def with_tiles(vals, tiles, sems, prepare):
    part = TILES // sems.shape[0]
    copies = [
        pltpu.make_async_copy(vals.at[pl.ds(k * part, part)], tiles.at[pl.ds(k * part, part)], sems.at[k])
        for k in range(TILES // part)
    ]
    for copy in copies:
        copy.start()
    tiles[TILES] = jnp.zeros((T, T), BF)
    prepare()
    for copy in copies:
        copy.wait()


def over_pairs(far, ids, steps_of, tiles, step):
    @pl.loop(0, steps_of[far])
    def _(q):
        ns = [far * SLOTS + (q * UNROLL + k) * 2 for k in range(UNROLL)]
        step([(n, jnp.concatenate([tiles[ids[n]], tiles[ids[n + 1]]], axis=0)) for n in ns])


def forward_prepare(panel, acc, lhs):
    acc[...] = jnp.zeros(acc.shape, F32)
    for s in range(NR):
        lhs[s, :H] = panel[s]
        lhs[s, H:] = jnp.ones((2 * DEG, T), BF)


def forward_sums(far, lists, tiles, acc, lhs):
    ids, slots, srcs, steps_of, _ = lists

    def step(pairs):
        prods = [dot(lhs[srcs[n]], pair, NT) for n, pair in pairs]
        for (n, _), prod in zip(pairs, prods):
            for k in range(2):
                slot = slots[n + k]
                acc[slot] = acc[slot] + prod[: H + DEG, k * T : (k + 1) * T]

    over_pairs(far, ids, steps_of, tiles, step)


def forward_far_kernel(*refs):
    *lists, vals, panel, out, tiles, acc, lhs, sems = refs
    with_tiles(vals, tiles, sems, lambda: forward_prepare(panel, acc, lhs))
    forward_sums(1, lists, tiles, acc, lhs)

    @pl.loop(0, HALF, unroll=4)
    def _(b):
        out[b, :H] = acc[b, :H].astype(BF)
        out[b, H:] = two_parts(acc[b, H:])


def forward_near_kernel(*refs):
    *lists, tiles, panel, out, lhs = refs
    forward_prepare(panel, out, lhs)
    forward_sums(0, lists, tiles, out, lhs)


COST = pl.CostEstimate(flops=64 * 2 * BLK * T * T, bytes_accessed=2**21, transcendentals=0)
LOADED = pltpu.VMEM((TILES + 1, T, T), BF)
SEMS = pltpu.SemaphoreType.DMA((4,))


def forward_far(lists, vals, panel):
    scratch = [pltpu.VMEM((HALF, H + DEG, T), F32), pltpu.VMEM((NR, BLK, T), BF), SEMS]
    out_shape = (pltpu.VMEM((HALF, BLK, T), BF), LOADED)
    return call(forward_far_kernel, "forward_far", out_shape, *lists, vals, panel, scratch=scratch, cost=COST)


def forward_near(lists, tiles, panel):
    scratch = [pltpu.VMEM((NR, BLK, T), BF)]
    out_shape = pltpu.VMEM((HALF, H + DEG, T), F32)
    return call(forward_near_kernel, "forward_near", out_shape, *lists, tiles, panel, scratch=scratch, cost=COST)


def core_sum_kernel(near, other, out):
    @pl.loop(0, NB)
    def _(z):
        for x in range(NP):
            sums, deg = add_blocks([near[x * NB + z], other[x * NB + z]])
            out[x, z, :H] = sums.astype(BF)
            out[x, z, H:] = two_parts(deg)


def core_sum(near, other):
    return call(core_sum_kernel, "core_sum", pltpu.VMEM((NP, NB, BLK, T), BF), near, other)


def x_sum_kernel(parts, out):
    @pl.loop(0, NB)
    def _(z):
        sums, deg = add_blocks([parts[x, z] for x in range(NP)])
        out[z, :H] = sums.astype(BF)
        out[z, H:] = two_parts(deg)


def x_sum(parts):
    return call(x_sum_kernel, "x_sum", pltpu.VMEM((NB, BLK, T), BF), parts)


def node_kernel(cores, parts, feats, d_out, w_self, w_neigh, out_feats, d_sum, base, pairs):
    my_core = cores[0]
    sums, deg = add_blocks([parts[z] for z in range(NB)])
    deg = 1.0 + deg[:1]
    mean_t = (sums / deg).astype(BF)
    pre = dot(feats[...], w_self[...]) + dot(mean_t, w_neigh[...], TN)
    gate = jax.nn.sigmoid(pre)
    out_feats[...] = (pre * gate).astype(BF)
    d_pre = (d_out[...].astype(F32) * gate * (1.0 + pre * (1.0 - gate))).astype(BF)
    d_sum_t = (dot(w_neigh[...], d_pre, NT) / deg).astype(BF)
    for z in range(NB):
        d_sum[z, :H] = d_sum_t
    base[...] = dot(w_self[...], d_pre, NT)
    rows = GRAD // 2
    for part, grad in enumerate((dot(feats[...], d_pre, TN), dot(mean_t, d_pre))):
        for g in range(H // rows):
            pairs[g, part * rows : (part + 1) * rows] = grad[g * rows : (g + 1) * rows]
    for z in range(NB):
        for j in range(NP * NC):
            x, za, c = j // (NA * NC), j // NC % NA, j % NC
            d = (x * NA * NB + ((z * NA + za + my_core) & (NA * NB - 1))) * NC + c
            d_sum[z, H + j * GROWS : H + (j + 1) * GROWS] = fold(pairs[d]).astype(BF)


def node(cores, parts, feats, d_out, w_self, w_neigh):
    out_shape = (
        jax.ShapeDtypeStruct((T, H), BF),
        pltpu.VMEM((NB, H + NP * NC * GROWS, T), BF),
        pltpu.VMEM((H, T), F32),
    )
    scratch = [pltpu.VMEM((NP * NB * NC, GRAD, H), F32)]
    return call(node_kernel, "node", out_shape, cores, parts, feats, d_out, w_self, w_neigh, scratch=scratch)


def copies_kernel(parts, out):
    grads = jnp.zeros((NP * NC * GROWS, T), F32)
    for z in range(NB):
        grads = grads + parts[z, H:].astype(F32)
        for x in range(NP):
            out[x, z * H : (z + 1) * H] = parts[z, :H]
    for j in range(NP * NC):
        at = NB * H + j % NC * 2 * GROWS
        out[j // NC, at : at + 2 * GROWS] = two_parts(grads[j * GROWS : (j + 1) * GROWS])


def copies(parts):
    out_shape = pltpu.VMEM((NP, NB * H + NC * 2 * GROWS, T), BF)
    return call(copies_kernel, "copies", out_shape, parts)


def own_gradients(blocks, my_core):
    at = pl.multiple_of(NB * H + my_core * 2 * GROWS, 2 * GROWS)
    total = 0.0
    for x in range(NP):
        both = blocks[x, pl.ds(at, 2 * GROWS)].astype(F32)
        total = total + both[:GROWS] + both[GROWS:]
    return total


def backward_sums(far, lists, tiles, blocks, acc):
    ids, slots, srcs, steps_of, _ = lists

    def block(n):
        return blocks[slots[n] // NB, pl.ds(pl.multiple_of((slots[n] & (NB - 1)) * H, H), H)]

    def step(pairs):
        sides = [jnp.concatenate([block(n), block(n + 1)], axis=1) for n, _ in pairs]
        prods = [dot(side, pair) for side, (_, pair) in zip(sides, pairs)]
        for (n, _), prod in zip(pairs, prods):
            acc[srcs[n]] = acc[srcs[n]] + prod

    over_pairs(far, ids, steps_of, tiles, step)


def backward_near_kernel(*refs):
    *lists, tiles, blocks, out, grads = refs
    out[...] = jnp.zeros(out.shape, F32)
    grads[...] = own_gradients(blocks, lists[4][0])
    backward_sums(0, lists, tiles, blocks, out)


def backward_far_kernel(*refs):
    *lists, tiles, blocks, near, grads, out, acc = refs
    acc[...] = near[...]
    backward_sums(1, lists, tiles, blocks, acc)
    grad_rows = two_parts(grads[...] + own_gradients(blocks, lists[4][0]))
    for s in range(NR):
        out[s, :H] = acc[s].astype(BF)
        out[s, H:] = grad_rows


def backward_near(lists, tiles, blocks):
    out_shape = (pltpu.VMEM((NR, H, T), F32), pltpu.VMEM((GROWS, T), F32))
    return call(backward_near_kernel, "backward_near", out_shape, *lists, tiles, blocks, cost=COST)


def backward_far(lists, tiles, blocks, near, grads):
    scratch = [pltpu.VMEM((NR, H, T), F32)]
    out_shape = pltpu.VMEM((NR, H + 2 * GROWS, T), BF)
    args = (*lists, tiles, blocks, near, grads)
    return call(backward_far_kernel, "backward_far", out_shape, *args, scratch=scratch, cost=COST)


def final_kernel(parts, base, out, *grads):
    total = parts[0].astype(F32)
    for r in range(1, NR):
        total = total + parts[r].astype(F32)
    out[...] = (base[...] + total[:H]).T.astype(BF)
    rows = GRAD // 2
    for k in range(H // T):
        high, low = (total[H + (2 * p + k) * GRAD :][:GRAD] for p in range(2))
        for part, grad in enumerate(grads):
            grad[:, k * T : (k + 1) * T] = (high + low)[part * rows : (part + 1) * rows]


def final(parts, base):
    grad = jax.ShapeDtypeStruct((GRAD // 2, H), F32)
    return call(final_kernel, "final", (jax.ShapeDtypeStruct((T, H), BF), grad, grad), parts, base)


def dom_of(x, zb, za, c):
    return (x * NA * NB + (zb * NA + za + c) % (NA * NB)) * NC + c


FIRST = [[dom_of(x, b, a, c) for x in range(NX) for a in range(NA)] for b in range(NB) for c in range(NC)]
SECOND = [[dom_of(x, b, a, c) for b in range(NB)] for x in range(NX) for a in range(NA) for c in range(NC)]


def per_device(feats, w_self, w_neigh, tile_vals, tile_owner, tile_src, tile_count, d_out):
    tiles, owners, sources = tile_vals[0, 0], tile_owner[0, 0], tile_src[0, 0]
    my_core = (lax.axis_index("dom") % NC).reshape(1)
    swap = [(d, d ^ 1) for d in range(NP * NB * NC)]

    panel = lax.all_to_all(spread(feats), "rep", 0, 0)
    lists = (*order(owners, sources, tile_count[0], my_core), my_core)
    far, loaded = forward_far(lists, tiles, panel)
    near = forward_near(lists, loaded, panel)
    parts = core_sum(near, lax.ppermute(far, "dom", swap))
    parts = x_sum(lax.all_to_all(parts, "dom", 0, 0, axis_index_groups=FIRST))
    parts = lax.all_to_all(parts, "dom", 0, 0, axis_index_groups=SECOND)

    out_feats, d_sum, base = node(my_core, parts, feats, d_out, w_self, w_neigh)

    column = copies(lax.all_to_all(d_sum, "dom", 0, 0, axis_index_groups=SECOND))
    blocks = lax.all_to_all(column, "dom", 0, 0, axis_index_groups=FIRST)
    others = lax.ppermute(blocks, "dom", swap)
    back, grads = backward_near(lists, loaded, blocks)
    back = backward_far(lists, loaded, others, back, grads)
    return (out_feats, *final(lax.all_to_all(back, "rep", 0, 0), base))


def solution(mesh):
    in_specs = (
        P(("rep", "dom"), None),
        P(),
        P(),
        P("rep", "dom", None, None, None),
        P("rep", "dom", None),
        P("rep", "dom", None),
        P("rep", "dom"),
        P(("rep", "dom"), None),
    )
    out_specs = (P(("rep", "dom"), None), P(("rep", "dom"), None), P("dom", None), P("dom", None))
    return jax.shard_map(
        per_device, mesh=mesh, in_specs=in_specs, out_specs=out_specs, check_vma=False
    )
```

```python
import jax
import jax.numpy as jnp
from jax import lax
from jax.experimental import pallas as pl
from jax.experimental.pallas import tpu as pltpu
from jax.sharding import Mesh
from jax.sharding import PartitionSpec as P


BF = jnp.bfloat16
F32 = jnp.float32
NX, NB, NA, NC, NR = 4, 4, 2, 2, 8
NP = NX * NA
T = 128
H = 256
TILES = 128
SLOTS = 144
UNROLL = 8
HALF = NP * NB
DEG = 8
GRAD = 8
DROWS = 16
GROWS = 2 * GRAD
BLK = H + 2 * DEG
VMEM = pl.BlockSpec(memory_space=pltpu.VMEM)
SMEM = pl.BlockSpec(memory_space=pltpu.SMEM)
HBM = pl.BlockSpec(memory_space=pltpu.HBM)
PARAMS = pltpu.CompilerParams(vmem_limit_bytes=20 * 1024 * 1024)
NT = (((1,), (1,)), ((), ()))
TN = (((0,), (0,)), ((), ()))


def dot(a, b, dims=(((1,), (0,)), ((), ()))):
    return lax.dot_general(a, b, dims, preferred_element_type=F32)


def call(kernel, name, out_shape, *args, scratch=(), cost=None):
    def spec(a):
        return SMEM if a.dtype == jnp.int32 else HBM if a.shape == (TILES, T, T) else VMEM

    def place(a):
        s = spec(a)
        return a if s is SMEM else pltpu.with_memory_space_constraint(a, s.memory_space)

    args = [place(a) for a in args]
    return pl.pallas_call(
        kernel,
        in_specs=[spec(a) for a in args],
        out_specs=jax.tree.map(spec, out_shape, is_leaf=lambda a: hasattr(a, "dtype")),
        out_shape=out_shape,
        scratch_shapes=scratch,
        compiler_params=PARAMS,
        cost_estimate=cost,
        name=name,
    )(*args)


def add_blocks(blocks):
    sums, deg = 0.0, 0.0
    for block in blocks:
        block = block.astype(F32)
        sums = sums + block[:H]
        deg = deg + block[H : H + DEG]
        if block.shape[0] == BLK:
            deg = deg + block[H + DEG :]
    return sums, deg


def fold(rows):
    return jnp.concatenate([rows[:, k : k + T] for k in range(0, H, T)], axis=0)


def two_parts(rows):
    high = rows.astype(BF).astype(F32)
    return jnp.concatenate([high, rows - high], axis=0).astype(BF)


def order_kernel(owners, sources, counts, cores, ids, owner_slots, srcs, steps_of, seen):
    count, my_core = counts[0], cores[0]

    def bucket(t):
        return ((owners[t] & 1) ^ my_core) * NR + sources[t]

    @pl.loop(0, NC * NR)
    def _(b):
        seen[b] = 0

    @pl.loop(0, count)
    def _(t):
        seen[bucket(t)] = seen[bucket(t)] + 1

    for far in range(NC):
        at = jnp.int32(far * SLOTS)
        for src in range(NR):
            size = seen[far * NR + src]
            seen[far * NR + src] = at
            at = at + size

            @pl.when(size % 2 == 1)
            def _():
                ids[at], owner_slots[at], srcs[at] = TILES, 0, src

            at = at + size % 2
        size = at - far * SLOTS
        steps = (size + 2 * UNROLL - 1) // (2 * UNROLL)
        steps_of[far] = steps

        @pl.loop(size, steps * 2 * UNROLL)
        def _(k):
            ids[far * SLOTS + k], owner_slots[far * SLOTS + k], srcs[far * SLOTS + k] = TILES, 0, 0

    @pl.loop(0, count)
    def _(t):
        at = seen[bucket(t)]
        seen[bucket(t)] = at + 1
        ids[at] = t
        x, zb, za = owners[t] >> 4, (owners[t] >> 2) & 3, (owners[t] >> 1) & 1
        owner_slots[at] = (x * NA + za) * NB + zb
        srcs[at] = sources[t]


def order(owners, sources, counts, cores):
    lists = jax.ShapeDtypeStruct((NC * SLOTS,), jnp.int32)
    out_shape = (lists, lists, lists, jax.ShapeDtypeStruct((NC,), jnp.int32))
    scratch = [pltpu.SMEM((NC * NR,), jnp.int32)]
    return call(order_kernel, "order", out_shape, owners, sources, counts, cores, scratch=scratch)


def with_tiles(vals, tiles, sems, prepare):
    part = TILES // sems.shape[0]
    copies = [
        pltpu.make_async_copy(vals.at[pl.ds(k * part, part)], tiles.at[pl.ds(k * part, part)], sems.at[k])
        for k in range(TILES // part)
    ]
    for copy in copies:
        copy.start()
    tiles[TILES] = jnp.zeros((T, T), BF)
    prepare()
    for copy in copies:
        copy.wait()


def over_pairs(far, ids, steps_of, tiles, step):
    @pl.loop(0, steps_of[far])
    def _(q):
        ns = [far * SLOTS + (q * UNROLL + k) * 2 for k in range(UNROLL)]
        step([(n, jnp.concatenate([tiles[ids[n]], tiles[ids[n + 1]]], axis=0)) for n in ns])


def forward_prepare(panel, acc, lhs):
    acc[...] = jnp.zeros(acc.shape, F32)
    for s in range(NR):
        lhs[s, :H] = panel[s].astype(F32).T.astype(BF)
        lhs[s, H:] = jnp.ones((2 * DEG, T), BF)


def forward_sums(far, lists, tiles, acc, lhs):
    ids, slots, srcs, steps_of, _ = lists

    def step(pairs):
        prods = [dot(lhs[srcs[n]], pair, NT) for n, pair in pairs]
        for (n, _), prod in zip(pairs, prods):
            for k in range(2):
                slot = slots[n + k]
                acc[slot] = acc[slot] + prod[: H + DEG, k * T : (k + 1) * T]

    over_pairs(far, ids, steps_of, tiles, step)


def forward_far_kernel(*refs):
    *lists, vals, panel, out, tiles, lhs, acc, sems = refs
    with_tiles(vals, tiles, sems, lambda: forward_prepare(panel, acc, lhs))
    forward_sums(1, lists, tiles, acc, lhs)

    @pl.loop(0, HALF, unroll=4)
    def _(b):
        out[b, :H] = acc[b, :H].astype(BF)
        out[b, H:] = two_parts(acc[b, H:])


def forward_near_kernel(*refs):
    *lists, tiles, lhs, out = refs
    out[...] = jnp.zeros(out.shape, F32)
    forward_sums(0, lists, tiles, out, lhs)


COST = pl.CostEstimate(flops=64 * 2 * BLK * T * T, bytes_accessed=2**21, transcendentals=0)
LOADED = pltpu.VMEM((TILES + 1, T, T), BF)
SEMS = pltpu.SemaphoreType.DMA((4,))


def forward_far(lists, vals, panel):
    scratch = [pltpu.VMEM((HALF, H + DEG, T), F32), SEMS]
    out_shape = (pltpu.VMEM((HALF, BLK, T), BF), LOADED, pltpu.VMEM((NR, BLK, T), BF))
    return call(forward_far_kernel, "forward_far", out_shape, *lists, vals, panel, scratch=scratch, cost=COST)


def forward_near(lists, tiles, lhs):
    out_shape = pltpu.VMEM((HALF, H + DEG, T), F32)
    return call(forward_near_kernel, "forward_near", out_shape, *lists, tiles, lhs, cost=COST)


def core_sum_kernel(near, other, out):
    @pl.loop(0, NP)
    def _(p):
        degs = []
        for b in range(NB):
            sums, deg = add_blocks([near[p * NB + b], other[p * NB + b]])
            out[p, b * H : (b + 1) * H] = sums.astype(BF)
            degs.append(deg[:1])
        deg = jnp.concatenate(degs, axis=0)
        high = deg.astype(BF).astype(F32)
        rest = jnp.zeros((DROWS - 2 * NB, T), F32)
        out[p, NB * H :] = jnp.concatenate([high, deg - high, rest], axis=0).astype(BF)


def core_sum(near, other):
    return call(core_sum_kernel, "core_sum", pltpu.VMEM((NP, NB * H + DROWS, T), BF), near, other)


def x_sum_kernel(parts, out):
    degs = parts[0, NB * H :].astype(F32)
    for p in range(1, NP):
        degs = degs + parts[p, NB * H :].astype(F32)
    for b in range(NB):
        sums = parts[0, b * H : (b + 1) * H].astype(F32)
        for p in range(1, NP):
            sums = sums + parts[p, b * H : (b + 1) * H].astype(F32)
        out[b, :H] = sums.astype(BF)
        deg = degs[b : b + 1] + degs[NB + b : NB + b + 1]
        out[b, H:] = two_parts(jnp.broadcast_to(deg, (DEG, T)))


def x_sum(parts):
    return call(x_sum_kernel, "x_sum", pltpu.VMEM((NB, BLK, T), BF), parts)


def node_kernel(parts, feats, d_out, w_self, w_neigh, out_feats, d_sum, base, pairs):
    sums, deg = add_blocks([parts[z] for z in range(NB)])
    deg = 1.0 + deg[:1]
    mean_t = (sums / deg).astype(BF)
    pre = dot(feats[...], w_self[...]) + dot(mean_t, w_neigh[...], TN)
    gate = jax.nn.sigmoid(pre)
    out_feats[...] = (pre * gate).astype(BF)
    d_pre = (d_out[...].astype(F32) * gate * (1.0 + pre * (1.0 - gate))).astype(BF)
    d_sum_t = (dot(w_neigh[...], d_pre, NT) / deg).astype(BF)
    for z in range(NB):
        d_sum[z, :H] = d_sum_t
    base[...] = dot(w_self[...], d_pre, NT)
    rows = GRAD // 2
    for part, grad in enumerate((dot(feats[...], d_pre, TN), dot(mean_t, d_pre))):
        for g in range(H // rows):
            pairs[g, part * rows : (part + 1) * rows] = grad[g * rows : (g + 1) * rows]
    for z in range(NB):
        for j in range(NP * NC):
            x, za, c = j // (NA * NC), j // NC % NA, j % NC
            d = ((x * NB + z) * NA + za) * NC + c
            d_sum[z, H + j * GROWS : H + (j + 1) * GROWS] = fold(pairs[d]).astype(BF)


def node(parts, feats, d_out, w_self, w_neigh):
    out_shape = (
        jax.ShapeDtypeStruct((T, H), BF),
        pltpu.VMEM((NB, H + NP * NC * GROWS, T), BF),
        pltpu.VMEM((H, T), F32),
    )
    scratch = [pltpu.VMEM((NP * NB * NC, GRAD, H), F32)]
    return call(node_kernel, "node", out_shape, parts, feats, d_out, w_self, w_neigh, scratch=scratch)


def copies_kernel(parts, out):
    grads = jnp.zeros((NP * NC * GROWS, T), F32)
    for z in range(NB):
        grads = grads + parts[z, H:].astype(F32)
        for x in range(NP):
            out[x, z * H : (z + 1) * H] = parts[z, :H]
    for j in range(NP * NC):
        at = NB * H + j % NC * 2 * GROWS
        out[j // NC, at : at + 2 * GROWS] = two_parts(grads[j * GROWS : (j + 1) * GROWS])


def copies(parts):
    out_shape = pltpu.VMEM((NP, NB * H + NC * 2 * GROWS, T), BF)
    return call(copies_kernel, "copies", out_shape, parts)


def own_gradients(blocks, my_core):
    at = pl.multiple_of(NB * H + my_core * 2 * GROWS, 2 * GROWS)
    total = 0.0
    for x in range(NP):
        both = blocks[x, pl.ds(at, 2 * GROWS)].astype(F32)
        total = total + both[:GROWS] + both[GROWS:]
    return total


def backward_sums(far, lists, tiles, blocks, acc):
    ids, slots, srcs, steps_of, _ = lists

    def block(n):
        return blocks[slots[n] // NB, pl.ds(pl.multiple_of((slots[n] & (NB - 1)) * H, H), H)]

    def step(pairs):
        sides = [jnp.concatenate([block(n), block(n + 1)], axis=1) for n, _ in pairs]
        prods = [dot(side, pair) for side, (_, pair) in zip(sides, pairs)]
        for (n, _), prod in zip(pairs, prods):
            acc[srcs[n]] = acc[srcs[n]] + prod

    over_pairs(far, ids, steps_of, tiles, step)


def backward_near_kernel(*refs):
    *lists, tiles, blocks, out, grads = refs
    out[...] = jnp.zeros(out.shape, F32)
    grads[...] = own_gradients(blocks, lists[4][0])
    backward_sums(0, lists, tiles, blocks, out)


def backward_far_kernel(*refs):
    *lists, tiles, blocks, near, grads, out, acc = refs
    acc[...] = near[...]
    backward_sums(1, lists, tiles, blocks, acc)
    grad_rows = two_parts(grads[...] + own_gradients(blocks, lists[4][0]))
    for s in range(NR):
        out[s, :H] = acc[s].astype(BF)
        out[s, H:] = grad_rows


def backward_near(lists, tiles, blocks):
    out_shape = (pltpu.VMEM((NR, H, T), F32), pltpu.VMEM((GROWS, T), F32))
    return call(backward_near_kernel, "backward_near", out_shape, *lists, tiles, blocks, cost=COST)


def backward_far(lists, tiles, blocks, near, grads):
    scratch = [pltpu.VMEM((NR, H, T), F32)]
    out_shape = pltpu.VMEM((NR, H + 2 * GROWS, T), BF)
    args = (*lists, tiles, blocks, near, grads)
    return call(backward_far_kernel, "backward_far", out_shape, *args, scratch=scratch, cost=COST)


def final_kernel(parts, base, out, *grads):
    total = parts[0].astype(F32)
    for r in range(1, NR):
        total = total + parts[r].astype(F32)
    out[...] = (base[...] + total[:H]).T.astype(BF)
    rows = GRAD // 2
    for k in range(H // T):
        high, low = (total[H + (2 * p + k) * GRAD :][:GRAD] for p in range(2))
        for part, grad in enumerate(grads):
            grad[:, k * T : (k + 1) * T] = (high + low)[part * rows : (part + 1) * rows]


def final(parts, base):
    grad = jax.ShapeDtypeStruct((GRAD // 2, H), F32)
    return call(final_kernel, "final", (jax.ShapeDtypeStruct((T, H), BF), grad, grad), parts, base)


def shift(size, by):
    return [(i, (i + by) % size) for i in range(size)]


def per_device(feats, w_self, w_neigh, tile_vals, tile_owner, tile_src, tile_count, d_out):
    tiles, owners, sources = tile_vals[0, 0], tile_owner[0, 0], tile_src[0, 0]
    my_core = lax.axis_index("core").reshape(1)
    swap = shift(NC, 1)

    panel = lax.all_to_all(jnp.broadcast_to(feats, (NR, T, H)), "rep", 0, 0)
    lists = (*order(owners, sources, tile_count[0], my_core), my_core)
    far, loaded, lhs = forward_far(lists, tiles, panel)
    near = forward_near(lists, loaded, lhs)
    parts = core_sum(near, lax.ppermute(far, "core", swap))
    parts = x_sum(lax.all_to_all(parts, ("x", "za"), 0, 0))
    parts = lax.all_to_all(parts, "zb", 0, 0)

    out_feats, d_sum, base = node(parts, feats, d_out, w_self, w_neigh)

    column = copies(lax.all_to_all(d_sum, "zb", 0, 0))
    blocks = lax.all_to_all(column, ("x", "za"), 0, 0)
    others = lax.ppermute(blocks, "core", swap)
    back, grads = backward_near(lists, loaded, blocks)
    back = backward_far(lists, loaded, others, back, grads)
    return (out_feats, *final(lax.all_to_all(back, "rep", 0, 0), base))


def solution(mesh):
    split = Mesh(mesh.devices.reshape(NR, NX, NB, NA, NC), ("rep", "x", "zb", "za", "core"))
    dom = ("x", "zb", "za", "core")
    nodes = P(("rep", *dom), None)
    in_specs = (
        nodes,
        P(),
        P(),
        P("rep", dom, None, None, None),
        P("rep", dom, None),
        P("rep", dom, None),
        P("rep", dom),
        nodes,
    )
    out_specs = (nodes, nodes, P(dom, None), P(dom, None))
    return jax.shard_map(
        per_device, mesh=split, in_specs=in_specs, out_specs=out_specs, check_vma=False
    )
```

```python
import jax
import jax.numpy as jnp
from jax import lax
from jax.experimental import pallas as pl
from jax.experimental.pallas import tpu as pltpu
from jax.sharding import Mesh
from jax.sharding import PartitionSpec as P


BF = jnp.bfloat16
F32 = jnp.float32
NX, NB, NA, NC, NR = 4, 4, 2, 2, 8
NP = NX * NA
T = 128
H = 256
TILES = 128
EARLY = 64
SLOTS = 144
UNROLL = 8
HALF = NP * NB
DEG = 8
GRAD = 8
DROWS = 16
GROWS = 2 * GRAD
BLK = H + 2 * DEG
VMEM = pl.BlockSpec(memory_space=pltpu.VMEM)
SMEM = pl.BlockSpec(memory_space=pltpu.SMEM)
HBM = pl.BlockSpec(memory_space=pltpu.HBM)
PARAMS = pltpu.CompilerParams(vmem_limit_bytes=20 * 1024 * 1024)
NT = (((1,), (1,)), ((), ()))
TN = (((0,), (0,)), ((), ()))


def dot(a, b, dims=(((1,), (0,)), ((), ()))):
    return lax.dot_general(a, b, dims, preferred_element_type=F32)


def call(kernel, name, out_shape, *args, scratch=(), cost=None):
    def spec(a):
        return SMEM if a.dtype == jnp.int32 else HBM if a.shape == (TILES, T, T) else VMEM

    def place(a):
        s = spec(a)
        return a if s is SMEM else pltpu.with_memory_space_constraint(a, s.memory_space)

    args = [place(a) for a in args]
    return pl.pallas_call(
        kernel,
        in_specs=[spec(a) for a in args],
        out_specs=jax.tree.map(spec, out_shape, is_leaf=lambda a: hasattr(a, "dtype")),
        out_shape=out_shape,
        scratch_shapes=scratch,
        compiler_params=PARAMS,
        cost_estimate=cost,
        name=name,
    )(*args)


def add_blocks(blocks):
    sums, deg = 0.0, 0.0
    for block in blocks:
        block = block.astype(F32)
        sums = sums + block[:H]
        deg = deg + block[H : H + DEG]
        if block.shape[0] == BLK:
            deg = deg + block[H + DEG :]
    return sums, deg


def fold(rows):
    return jnp.concatenate([rows[:, k : k + T] for k in range(0, H, T)], axis=0)


def two_parts(rows):
    high = rows.astype(BF).astype(F32)
    return jnp.concatenate([high, rows - high], axis=0).astype(BF)


def order_kernel(owners, sources, counts, cores, vals, ids, owner_slots, srcs, steps_of, early, seen, sem):
    count, my_core = counts[0], cores[0]
    copy = pltpu.make_async_copy(vals.at[pl.ds(0, EARLY)], early, sem)
    copy.start()

    def bucket(t):
        return ((owners[t] & 1) ^ my_core) * NR + sources[t]

    @pl.loop(0, NC * NR)
    def _(b):
        seen[b] = 0

    @pl.loop(0, count)
    def _(t):
        seen[bucket(t)] = seen[bucket(t)] + 1

    for far in range(NC):
        at = jnp.int32(far * SLOTS)
        for src in range(NR):
            size = seen[far * NR + src]
            seen[far * NR + src] = at
            at = at + size

            @pl.when(size % 2 == 1)
            def _():
                ids[at], owner_slots[at], srcs[at] = TILES, 0, src

            at = at + size % 2
        size = at - far * SLOTS
        steps = (size + 2 * UNROLL - 1) // (2 * UNROLL)
        steps_of[far] = steps

        @pl.loop(size, steps * 2 * UNROLL)
        def _(k):
            ids[far * SLOTS + k], owner_slots[far * SLOTS + k], srcs[far * SLOTS + k] = TILES, 0, 0

    @pl.loop(0, count)
    def _(t):
        at = seen[bucket(t)]
        seen[bucket(t)] = at + 1
        ids[at] = t
        x, zb, za = owners[t] >> 4, (owners[t] >> 2) & 3, (owners[t] >> 1) & 1
        owner_slots[at] = (x * NA + za) * NB + zb
        srcs[at] = sources[t]

    copy.wait()


def order(owners, sources, counts, cores, vals):
    lists = jax.ShapeDtypeStruct((NC * SLOTS,), jnp.int32)
    out_shape = (lists, lists, lists, jax.ShapeDtypeStruct((NC,), jnp.int32), pltpu.VMEM((EARLY, T, T), BF))
    scratch = [pltpu.SMEM((NC * NR,), jnp.int32), pltpu.SemaphoreType.DMA]
    return call(order_kernel, "order", out_shape, owners, sources, counts, cores, vals, scratch=scratch)


def with_tiles(early, vals, tiles, sems, prepare):
    part = (TILES - EARLY) // sems.shape[0]
    copies = [
        pltpu.make_async_copy(vals.at[pl.ds(at, part)], tiles.at[pl.ds(at, part)], sems.at[k])
        for k, at in enumerate(range(EARLY, TILES, part))
    ]
    for copy in copies:
        copy.start()
    tiles[:EARLY] = early[...]
    tiles[TILES] = jnp.zeros((T, T), BF)
    prepare()
    for copy in copies:
        copy.wait()


def over_pairs(far, ids, steps_of, tiles, step):
    @pl.loop(0, steps_of[far])
    def _(q):
        ns = [far * SLOTS + (q * UNROLL + k) * 2 for k in range(UNROLL)]
        step([(n, jnp.concatenate([tiles[ids[n]], tiles[ids[n + 1]]], axis=0)) for n in ns])


def forward_prepare(panel, acc, lhs):
    acc[...] = jnp.zeros(acc.shape, F32)
    for s in range(NR):
        lhs[s, :H] = panel[s].astype(F32).T.astype(BF)
        lhs[s, H:] = jnp.ones((2 * DEG, T), BF)


def forward_sums(far, lists, tiles, acc, lhs):
    ids, slots, srcs, steps_of, _ = lists

    def step(pairs):
        prods = [dot(lhs[srcs[n]], pair, NT) for n, pair in pairs]
        for (n, _), prod in zip(pairs, prods):
            for k in range(2):
                slot = slots[n + k]
                acc[slot] = acc[slot] + prod[: H + DEG, k * T : (k + 1) * T]

    over_pairs(far, ids, steps_of, tiles, step)


def forward_far_kernel(*refs):
    *lists, early, vals, panel, out, tiles, lhs, acc, sems = refs
    with_tiles(early, vals, tiles, sems, lambda: forward_prepare(panel, acc, lhs))
    forward_sums(1, lists, tiles, acc, lhs)

    @pl.loop(0, HALF, unroll=4)
    def _(b):
        out[b, :H] = acc[b, :H].astype(BF)
        out[b, H:] = two_parts(acc[b, H:])


def forward_near_kernel(*refs):
    *lists, tiles, lhs, out = refs
    out[...] = jnp.zeros(out.shape, F32)
    forward_sums(0, lists, tiles, out, lhs)


COST = pl.CostEstimate(flops=64 * 2 * BLK * T * T, bytes_accessed=2**21, transcendentals=0)
LOADED = pltpu.VMEM((TILES + 1, T, T), BF)
SEMS = pltpu.SemaphoreType.DMA((4,))


def forward_far(lists, early, vals, panel):
    scratch = [pltpu.VMEM((HALF, H + DEG, T), F32), SEMS]
    out_shape = (pltpu.VMEM((HALF, BLK, T), BF), LOADED, pltpu.VMEM((NR, BLK, T), BF))
    return call(forward_far_kernel, "forward_far", out_shape, *lists, early, vals, panel, scratch=scratch, cost=COST)


def forward_near(lists, tiles, lhs):
    out_shape = pltpu.VMEM((HALF, H + DEG, T), F32)
    return call(forward_near_kernel, "forward_near", out_shape, *lists, tiles, lhs, cost=COST)


def core_sum_kernel(near, other, out):
    @pl.loop(0, NP)
    def _(p):
        degs = []
        for b in range(NB):
            sums, deg = add_blocks([near[p * NB + b], other[p * NB + b]])
            out[p, b * H : (b + 1) * H] = sums.astype(BF)
            degs.append(deg[:1])
        deg = jnp.concatenate(degs, axis=0)
        high = deg.astype(BF).astype(F32)
        rest = jnp.zeros((DROWS - 2 * NB, T), F32)
        out[p, NB * H :] = jnp.concatenate([high, deg - high, rest], axis=0).astype(BF)


def core_sum(near, other):
    return call(core_sum_kernel, "core_sum", pltpu.VMEM((NP, NB * H + DROWS, T), BF), near, other)


def x_sum_kernel(parts, out):
    degs = parts[0, NB * H :].astype(F32)
    for p in range(1, NP):
        degs = degs + parts[p, NB * H :].astype(F32)
    for b in range(NB):
        sums = parts[0, b * H : (b + 1) * H].astype(F32)
        for p in range(1, NP):
            sums = sums + parts[p, b * H : (b + 1) * H].astype(F32)
        out[b, :H] = sums.astype(BF)
        deg = degs[b : b + 1] + degs[NB + b : NB + b + 1]
        out[b, H:] = two_parts(jnp.broadcast_to(deg, (DEG, T)))


def x_sum(parts):
    return call(x_sum_kernel, "x_sum", pltpu.VMEM((NB, BLK, T), BF), parts)


def node_kernel(parts, feats, d_out, w_self, w_neigh, out_feats, d_sum, base, pairs):
    sums, deg = add_blocks([parts[z] for z in range(NB)])
    deg = 1.0 + deg[:1]
    mean_t = (sums / deg).astype(BF)
    pre = dot(feats[...], w_self[...]) + dot(mean_t, w_neigh[...], TN)
    gate = jax.nn.sigmoid(pre)
    out_feats[...] = (pre * gate).astype(BF)
    d_pre = (d_out[...].astype(F32) * gate * (1.0 + pre * (1.0 - gate))).astype(BF)
    d_sum_t = (dot(w_neigh[...], d_pre, NT) / deg).astype(BF)
    for z in range(NB):
        d_sum[z, :H] = d_sum_t
    base[...] = dot(w_self[...], d_pre, NT)
    rows = GRAD // 2
    for part, grad in enumerate((dot(feats[...], d_pre, TN), dot(mean_t, d_pre))):
        for g in range(H // rows):
            pairs[g, part * rows : (part + 1) * rows] = grad[g * rows : (g + 1) * rows]
    for z in range(NB):
        for j in range(NP * NC):
            x, za, c = j // (NA * NC), j // NC % NA, j % NC
            d = ((x * NB + z) * NA + za) * NC + c
            d_sum[z, H + j * GROWS : H + (j + 1) * GROWS] = fold(pairs[d]).astype(BF)


def node(parts, feats, d_out, w_self, w_neigh):
    out_shape = (
        jax.ShapeDtypeStruct((T, H), BF),
        pltpu.VMEM((NB, H + NP * NC * GROWS, T), BF),
        pltpu.VMEM((H, T), F32),
    )
    scratch = [pltpu.VMEM((NP * NB * NC, GRAD, H), F32)]
    return call(node_kernel, "node", out_shape, parts, feats, d_out, w_self, w_neigh, scratch=scratch)


def copies_kernel(parts, out):
    grads = jnp.zeros((NP * NC * GROWS, T), F32)
    for z in range(NB):
        grads = grads + parts[z, H:].astype(F32)
        for x in range(NP):
            out[x, z * H : (z + 1) * H] = parts[z, :H]
    for j in range(NP * NC):
        at = NB * H + j % NC * 2 * GROWS
        out[j // NC, at : at + 2 * GROWS] = two_parts(grads[j * GROWS : (j + 1) * GROWS])


def copies(parts):
    out_shape = pltpu.VMEM((NP, NB * H + NC * 2 * GROWS, T), BF)
    return call(copies_kernel, "copies", out_shape, parts)


def own_gradients(blocks, my_core):
    at = pl.multiple_of(NB * H + my_core * 2 * GROWS, 2 * GROWS)
    total = 0.0
    for x in range(NP):
        both = blocks[x, pl.ds(at, 2 * GROWS)].astype(F32)
        total = total + both[:GROWS] + both[GROWS:]
    return total


def backward_sums(far, lists, tiles, blocks, acc):
    ids, slots, srcs, steps_of, _ = lists

    def block(n):
        return blocks[slots[n] // NB, pl.ds(pl.multiple_of((slots[n] & (NB - 1)) * H, H), H)]

    def step(pairs):
        sides = [jnp.concatenate([block(n), block(n + 1)], axis=1) for n, _ in pairs]
        prods = [dot(side, pair) for side, (_, pair) in zip(sides, pairs)]
        for (n, _), prod in zip(pairs, prods):
            acc[srcs[n]] = acc[srcs[n]] + prod

    over_pairs(far, ids, steps_of, tiles, step)


def backward_near_kernel(*refs):
    *lists, tiles, blocks, out, grads = refs
    out[...] = jnp.zeros(out.shape, F32)
    grads[...] = own_gradients(blocks, lists[4][0])
    backward_sums(0, lists, tiles, blocks, out)


def backward_far_kernel(*refs):
    *lists, tiles, blocks, near, grads, out, acc = refs
    acc[...] = near[...]
    backward_sums(1, lists, tiles, blocks, acc)
    grad_rows = two_parts(grads[...] + own_gradients(blocks, lists[4][0]))
    for s in range(NR):
        out[s, :H] = acc[s].astype(BF)
        out[s, H:] = grad_rows


def backward_near(lists, tiles, blocks):
    out_shape = (pltpu.VMEM((NR, H, T), F32), pltpu.VMEM((GROWS, T), F32))
    return call(backward_near_kernel, "backward_near", out_shape, *lists, tiles, blocks, cost=COST)


def backward_far(lists, tiles, blocks, near, grads):
    scratch = [pltpu.VMEM((NR, H, T), F32)]
    out_shape = pltpu.VMEM((NR, H + 2 * GROWS, T), BF)
    args = (*lists, tiles, blocks, near, grads)
    return call(backward_far_kernel, "backward_far", out_shape, *args, scratch=scratch, cost=COST)


def final_kernel(parts, base, out, *grads):
    total = parts[0].astype(F32)
    for r in range(1, NR):
        total = total + parts[r].astype(F32)
    out[...] = (base[...] + total[:H]).T.astype(BF)
    rows = GRAD // 2
    for k in range(H // T):
        high, low = (total[H + (2 * p + k) * GRAD :][:GRAD] for p in range(2))
        for part, grad in enumerate(grads):
            grad[:, k * T : (k + 1) * T] = (high + low)[part * rows : (part + 1) * rows]


def final(parts, base):
    grad = jax.ShapeDtypeStruct((GRAD // 2, H), F32)
    return call(final_kernel, "final", (jax.ShapeDtypeStruct((T, H), BF), grad, grad), parts, base)


def shift(size, by):
    return [(i, (i + by) % size) for i in range(size)]


def per_device(feats, w_self, w_neigh, tile_vals, tile_owner, tile_src, tile_count, d_out):
    tiles, owners, sources = tile_vals[0, 0], tile_owner[0, 0], tile_src[0, 0]
    my_core = lax.axis_index("core").reshape(1)
    swap = shift(NC, 1)

    panel = lax.all_to_all(jnp.broadcast_to(feats, (NR, T, H)), "rep", 0, 0)
    *lists, early = order(owners, sources, tile_count[0], my_core, tiles)
    lists = (*lists, my_core)
    far, loaded, lhs = forward_far(lists, early, tiles, panel)
    near = forward_near(lists, loaded, lhs)
    parts = core_sum(near, lax.ppermute(far, "core", swap))
    parts = x_sum(lax.all_to_all(parts, ("x", "za"), 0, 0))
    parts = lax.all_to_all(parts, "zb", 0, 0)

    out_feats, d_sum, base = node(parts, feats, d_out, w_self, w_neigh)

    column = copies(lax.all_to_all(d_sum, "zb", 0, 0))
    blocks = lax.all_to_all(column, ("x", "za"), 0, 0)
    others = lax.ppermute(blocks, "core", swap)
    back, grads = backward_near(lists, loaded, blocks)
    back = backward_far(lists, loaded, others, back, grads)
    return (out_feats, *final(lax.all_to_all(back, "rep", 0, 0), base))


def solution(mesh):
    split = Mesh(mesh.devices.reshape(NR, NX, NB, NA, NC), ("rep", "x", "zb", "za", "core"))
    dom = ("x", "zb", "za", "core")
    nodes = P(("rep", *dom), None)
    in_specs = (
        nodes,
        P(),
        P(),
        P("rep", dom, None, None, None),
        P("rep", dom, None),
        P("rep", dom, None),
        P("rep", dom),
        nodes,
    )
    out_specs = (nodes, nodes, P(dom, None), P(dom, None))
    return jax.shard_map(
        per_device, mesh=split, in_specs=in_specs, out_specs=out_specs, check_vma=False
    )
```
